256 devices in a mesh: tok: 64 (over y, z, core), grp: 4 (over x).
Axes of the slice: x: 4, y: 4, z: 8, core: 2. Of those that a mesh axis runs over, the one named last changes fastest.
Arguments:
- tokens: bfloat16 [98304, 1024], P(('tok', 'grp')), may hold values from -6 to 6
- norm_gain: float32 [1024], replicated, may hold values from 0.25 to 1.75
- input_weight: bfloat16 [1024, 3072], P('tok', 'grp')
- output_weight: bfloat16 [1024, 1024], P('tok', 'grp'), may hold values from -2 to 2
- segment_ids: int32 [98304], replicated, may hold values from 0 to 191, never falling along the last dimension, each value on 1 to 1024 neighbouring positions
- page_owner: int32 [24576, 1], P(('tok', 'grp')), may hold values from 0 to 63; in each aligned block of 96 rows (0 to 95, 96 to 191, ...) at most 3 rows name the same one
Outputs:
- attended: bfloat16 [98304, 1024], P(('tok', 'grp'))
- cache_pages: bfloat16 [49152, 8192], P(('tok', 'grp'))
The draws below stay inside these ranges and needn't reach their ends.
Inputs may be any that keep to these rules, and one draw needn't show every extreme that they name: `segment_ids`: segment ids never fall along the pack; every id occurs on 1 to 1024 consecutive tokens, and some document has exactly 1024 tokens. `page_owner`: within the 96 pages of one device no owner is named more than 3 times, and in some device one owner is named exactly 3 times.
All inputs are finite; a program needn't handle non-finite values.
Results may differ from the reference program's by a relative error of at most 0.0089.
Values may be sent and summed in bfloat16 or wider, within the bound.
A program may use at most 128 MiB of HBM per device.

```python
import math
import jax
import jax.numpy as jnp
import numpy as np
from jax import lax

D = 1024
H = 16
TOK_DEV = 384
SPAN = 1024
PAGE = 4
TOKENS = 98304
DOCS = 192
PAGES_DEV = 96
PAGES = 24576
CAP = 3
REACH = 3
N_TOK = 64
N_GRP = 4


def draw_input_weight(key, part):
    first_key = jax.random.fold_in(jax.random.fold_in(key, 11), 0)
    entries = jax.random.normal(first_key, (D, 3 * D), jnp.float32) * D ** (-0.5)
    return entries.astype(jnp.bfloat16)


def levels(stream_key, dims, cuts, low, largest):
    def one(axis_at, shards_of):
        draws = jax.random.uniform(jax.random.fold_in(jax.random.fold_in(stream_key, 6), axis_at), (shards_of,), jnp.float32, low / len(cuts), largest / len(cuts))
        return jnp.repeat(jnp.exp(draws), dims[axis_at] // shards_of).reshape((-1,) + (1,) * (len(dims) - axis_at - 1))

    level = one(*cuts[0])
    for cut in cuts[1:]:
        level = level * one(*cut)
    return level


def length_profile(amount, total, bound, slope):
    weights = [(1 << 20) // math.isqrt(standing ** slope) + 1 for standing in range(2, amount + 1)]
    rest, counts = total - bound - (amount - 1), [1] * (amount - 1)
    while rest > 0:
        free = [i for i in range(amount - 1) if counts[i] < bound]
        whole, budget = sum([weights[i] for i in free]), rest
        for i in free:
            more = min(bound - counts[i], max(1, budget * weights[i] // whole), rest)
            counts[i] = counts[i] + more
            rest = rest - more
    return np.array([bound] + counts)


def ragged(rng, count, total, most, skew):
    if count == 2:
        one = jax.random.randint(rng, (), max(1, total - most), min(most, total - 1) + 1)
        return jnp.stack([one, total - one])
    tallies = jnp.asarray(length_profile(count, total, most, skew), jnp.int32)
    couples = (count - 1) // 2
    giver, receiver = tallies[1:1 + 2 * couples:2], tallies[2:2 + 2 * couples:2]
    room = jnp.minimum(giver - 1, most - receiver)
    shifted = jax.random.randint(jax.random.fold_in(rng, 1), (couples,), 0, 1 << 20) % (room + 1)
    tallies = tallies.at[1:1 + 2 * couples:2].set(giver - shifted).at[2:2 + 2 * couples:2].set(receiver + shifted)
    return tallies[jax.random.permutation(jax.random.fold_in(rng, 2), count)]


def shared_out(rng, own, number, rows, number_of, top, limit, skew):
    order = jax.random.permutation(rng, number_of)
    heavy_load, ordinary = load_shares(number_of, rows * top, limit, skew, True), load_shares(number_of, rows * top, limit, skew, False)
    places = jnp.arange(number_of)

    def named(lengths, turn):
        used = int((lengths > 0).sum())
        fixed = max(1, used // 4)
        moved = fixed + (places - fixed + turn * (used - fixed)) % max(1, number_of - fixed)
        return jnp.zeros((number_of,), jnp.int32).at[order[jnp.where(places < fixed, places, moved)]].set(jnp.asarray(lengths, jnp.int32))

    lengths = jnp.where(number % 4 == 0, named(heavy_load, number // 4), named(ordinary, number - number // 4 - 1))
    mixed = jax.random.permutation(jax.random.fold_in(own, 3), number_of)
    donor, taker = mixed[0:number_of // 2 * 2:2], mixed[1:number_of // 2 * 2:2]
    slack = jnp.minimum(lengths[donor] - 1, limit - lengths[taker]) // 2
    slack = jnp.where((donor == order[0]) | (taker == order[0]) | (lengths[taker] == 0), 0, jnp.maximum(slack, 0))
    moved = jax.random.randint(jax.random.fold_in(own, 4), (number_of // 2,), 0, 1 << 20) % (slack + 1)
    lengths = lengths.at[donor].add(-moved).at[taker].add(moved)
    members = jnp.searchsorted(jnp.cumsum(lengths), jnp.arange(rows * top), side="right").astype(jnp.int32)
    table = members.reshape(top, rows).T
    table = table[jax.random.permutation(jax.random.fold_in(own, 1), rows)]
    turn = jax.random.randint(jax.random.fold_in(own, 2), (rows, 1), 0, top)
    return jnp.take_along_axis(table, (jnp.arange(top)[None, :] + turn) % top, axis=1)


def load_shares(amount, total, most, lean, full):
    portions = [(1 << 20) // math.isqrt(standing ** lean) + 1 for standing in range(1, amount + 1)]
    largest = most if full else min(most, max(-(-total // amount), total * portions[0] // sum(portions)))
    least = 1 if total - largest >= amount - 1 else 0
    counts, rest = [largest] + [least] * (amount - 1), total - largest - least * (amount - 1)
    while rest > 0:
        movable = [i for i in range(1, amount) if counts[i] < largest] or [i for i in range(1, amount) if counts[i] < most]
        mass, budget = sum([portions[i] for i in movable]), rest
        for i in movable:
            more = min(most - counts[i], max(1, budget * portions[i] // mass), rest)
            counts[i] = counts[i] + more
            rest = rest - more
    return np.array(counts)


def centred(key, extent, width, bound, pieces=(), kind=jnp.bfloat16):
    level = levels(key, extent, pieces, -0.22, 0.18) if pieces else 1.0
    array = jax.random.normal(key, extent, jnp.float32) * width * level
    return jnp.minimum(jnp.maximum(array, -bound), bound).astype(kind)


def setup_inputs(seed: int = 0) -> dict:
    key_list = jax.random.split(jax.random.key(seed), 7)
    tokens = centred(key_list[0], (TOKENS, D), 1.0, 6.0, ((0, 256),))
    norm_gain = jnp.clip(1.0 + 0.15 * jax.random.normal(key_list[1], (D,), jnp.float32), 0.25, 1.75)
    input_weight = draw_input_weight(jax.random.fold_in(key_list[6], 71), 0)
    output_weight = centred(key_list[3], (D, D), (max(1, D // 128)) ** -0.5, 2.0, ((0, 64), (1, 4)))
    segment_ids = jnp.searchsorted(jnp.cumsum(ragged(key_list[4], DOCS, TOKENS, SPAN, 2)), jnp.arange(TOKENS), side="right").astype(jnp.int32)
    page_owner_keys = jax.random.split(jax.random.fold_in(key_list[5], 1), PAGES // PAGES_DEV)
    page_owner_turns = jax.random.permutation(jax.random.fold_in(key_list[5], 3), PAGES // PAGES_DEV)
    page_owner = jax.vmap(lambda own, number: shared_out(jax.random.fold_in(key_list[5], 2), own, number, PAGES_DEV, N_TOK, 1, CAP, 2))(page_owner_keys, page_owner_turns).reshape((PAGES, 1))
    return {"tokens": tokens, "norm_gain": norm_gain, "input_weight": input_weight, "output_weight": output_weight, "segment_ids": segment_ids, "page_owner": page_owner}


NEG_FILL = -1e+30
ROPE_BASE = 160000.0
EPSILON = 1e-05

def layer_norm(tokens, norm_gain):
    values = tokens.astype(jnp.float32)
    center = lax.optimization_barrier(jnp.mean(values, axis=-1, keepdims=True))
    spread = lax.optimization_barrier(jnp.mean(jnp.square(values - center), axis=-1, keepdims=True))
    return ((values - center) * lax.rsqrt(spread + EPSILON) * norm_gain.astype(jnp.float32)).astype(jnp.bfloat16)

def rotate(block_part, positions, head_count):
    row_count = block_part.shape[0]
    head_dim = block_part.shape[1] // head_count
    half_dim = head_dim // 2
    shaped = block_part.reshape(row_count, head_count, head_dim)
    inverse = 1.0 / ROPE_BASE ** (jnp.arange(half_dim, dtype=jnp.float32) * 2.0 / head_dim)
    angles = positions.astype(jnp.float32)[:, None] * inverse[None, :]
    cosine = jnp.concatenate([jnp.cos(angles), jnp.cos(angles)], axis=1)[:, None, :]
    sine_table = jnp.concatenate([jnp.sin(angles), jnp.sin(angles)], axis=1)[:, None, :]
    turned = jnp.concatenate([-shaped[..., half_dim:], shaped[..., :half_dim]], axis=-1)
    return (shaped * cosine + turned * sine_table).reshape(row_count, head_count * head_dim).astype(jnp.bfloat16)

def positions_of(segment_ids, own_ids, first_row):
    starts = jnp.searchsorted(segment_ids, own_ids, side='left').astype(jnp.int32)
    return first_row + jnp.arange(own_ids.shape[0], dtype=jnp.int32) - starts

def attend_block(queries, key_window, value_window, query_ids, window_ids, head_count):
    row_count = queries.shape[0]
    window_len = key_window.shape[0]
    head_dim = queries.shape[1] // head_count
    score_scale = head_dim ** (-0.5)
    query_heads = queries.reshape(row_count, head_count, head_dim).astype(jnp.float32)
    key_heads = key_window.reshape(window_len, head_count, head_dim).astype(jnp.float32)
    value_heads = value_window.reshape(window_len, head_count, head_dim).astype(jnp.float32)
    scores = jnp.einsum('tnd,snd->nts', query_heads, key_heads) * score_scale
    allowed = query_ids[:, None] == window_ids[None, :]
    scores = jnp.where(allowed[None], scores, NEG_FILL)
    row_peak = lax.optimization_barrier(jnp.max(scores, axis=-1, keepdims=True))
    exponent = jnp.exp(scores - row_peak)
    row_total = lax.optimization_barrier(jnp.sum(exponent, axis=-1))
    weights = exponent.astype(jnp.bfloat16)
    mixed_rows = jnp.einsum('nts,snd->tnd', weights.astype(jnp.float32), value_heads)
    mixed_rows = mixed_rows / jnp.transpose(row_total)[:, :, None]
    return mixed_rows.reshape(row_count, head_count * head_dim).astype(jnp.bfloat16)

def reference(tokens, norm_gain, input_weight, output_weight, segment_ids, page_owner):
    device_count = N_TOK * N_GRP
    normed = layer_norm(tokens, norm_gain)

    def project(block_index):
        first_row = block_index * TOK_DEV
        row_block = lax.dynamic_slice_in_dim(normed, first_row, TOK_DEV, 0)
        joined = jnp.dot(row_block, input_weight, preferred_element_type=jnp.float32)
        own_ids = lax.dynamic_slice_in_dim(segment_ids, first_row, TOK_DEV, 0)
        positions = positions_of(segment_ids, own_ids, first_row)
        queries = rotate(joined[:, :D], positions, H)
        key_rows = rotate(joined[:, D:2 * D], positions, H)
        value_rows = joined[:, 2 * D:].astype(jnp.bfloat16)
        return (queries, key_rows, value_rows)
    indices = jnp.arange(device_count, dtype=jnp.int32)
    queries, key_rows, value_rows = lax.map(project, indices)
    keys_flat = key_rows.reshape(TOKENS, D)
    values_flat = value_rows.reshape(TOKENS, D)
    margin = REACH * TOK_DEV
    keys_pad = jnp.pad(keys_flat, ((margin, margin), (0, 0)))
    values_pad = jnp.pad(values_flat, ((margin, margin), (0, 0)))
    ids_pad = jnp.pad(segment_ids, (margin, margin), constant_values=-1)
    window_len = (2 * REACH + 1) * TOK_DEV

    def attend_one(operands):
        block_index, query_block = operands
        first_row = block_index * TOK_DEV
        key_window = lax.dynamic_slice_in_dim(keys_pad, first_row, window_len, 0)
        value_window = lax.dynamic_slice_in_dim(values_pad, first_row, window_len, 0)
        window_ids = lax.dynamic_slice_in_dim(ids_pad, first_row, window_len, 0)
        query_ids = lax.dynamic_slice_in_dim(segment_ids, first_row, TOK_DEV, 0)
        return attend_block(query_block, key_window, value_window, query_ids, window_ids, H)
    mixed_all = lax.map(attend_one, (indices, queries)).reshape(TOKENS, D)
    attended = jnp.dot(mixed_all, output_weight, preferred_element_type=jnp.float32).astype(jnp.bfloat16)
    page_rows = jnp.concatenate([keys_flat, values_flat], axis=1).reshape(PAGES, 2 * PAGE * D)
    owners = page_owner[:, 0].reshape(device_count, PAGES_DEV)
    same_owner = owners[:, :, None] == owners[:, None, :]
    earlier_mask = jnp.arange(PAGES_DEV)[:, None] > jnp.arange(PAGES_DEV)[None, :]
    page_ranks = lax.optimization_barrier(jnp.sum((same_owner & earlier_mask[None]).astype(jnp.int32), axis=2))
    source = jnp.arange(device_count, dtype=jnp.int32)[:, None]
    target = (owners * N_GRP + source % N_GRP) * (N_TOK * CAP) + source // N_GRP * CAP + page_ranks
    cache_pages = jnp.zeros((device_count * N_TOK * CAP, 2 * PAGE * D), jnp.bfloat16)
    cache_pages = cache_pages.at[target.reshape(-1)].set(page_rows)
    return (attended, cache_pages)
```

```python
import functools

import jax
import jax.numpy as jnp
import ml_dtypes
import numpy as np
from jax import lax
from jax.experimental import pallas as pl
from jax.experimental.pallas import tpu as pltpu
from jax.sharding import PartitionSpec as P

D = 1024
H = 16
SPAN = 1024
PAGE = 4
CAP = 3
BLK = 384
REACH = 3
WIN = (2 * REACH + 1) * BLK
EXTRA = 256
NEG_FILL = -1e30
ROPE_BASE = 160000.0
EPSILON = 1e-5
N_TOK = 64
NY, NZ = 4, 8
ROWS = 16
TOP = 1 << 30

MESH = pl.DeviceIdType.MESH
ANY = pl.BlockSpec(memory_space=pl.ANY)
VMEM = pl.BlockSpec(memory_space=pltpu.VMEM)
SMEM = pl.BlockSpec(memory_space=pltpu.SMEM)
BF, F32 = jnp.bfloat16, jnp.float32


def rope_tables():
    freq = 1.0 / ROPE_BASE ** (np.arange(32) * 2.0 / 64)
    lanes = np.tile(freq, 4)
    out = []
    for step in (32.0, 1.0):
        angle = step * np.arange(32)[:, None] * lanes[None, :]
        rest = np.concatenate([np.cos(angle), np.sin(angle)], axis=1)
        terms = []
        for _ in range(3):
            term = rest.astype(ml_dtypes.bfloat16)
            terms.append(term)
            rest = rest - term.astype(np.float64)
        out.append(np.concatenate(terms, axis=1))
    return np.stack(out)


def mm(left, right):
    return jnp.dot(left, right, preferred_element_type=F32)


def layer_norm(values, gain):
    center = jnp.mean(values, axis=-1, keepdims=True)
    moved = values - center
    spread = jnp.mean(jnp.square(moved), axis=-1, keepdims=True)
    return moved * lax.rsqrt(spread + EPSILON) * gain


def iota(shape, axis):
    return lax.broadcasted_iota(jnp.int32, shape, axis)


def column(row):
    eye = iota((128, 128), 0) == iota((128, 128), 1)
    return jnp.sum(jnp.where(eye, jnp.broadcast_to(row, (128, 128)), 0.0), axis=1, keepdims=True)


def ids_and_places(ids_ref, chunk):
    base = pl.multiple_of(chunk * 128, 128)
    own = ids_ref[:, pl.ds(pl.multiple_of(base + SPAN, 128), 128)].astype(F32)
    col = column(own)
    total = jnp.zeros((128, 128), F32)
    for k in range(SPAN // 128 + 1):
        part = ids_ref[:, pl.ds(pl.multiple_of(base + k * 128, 128), 128)].astype(F32)
        total = total + jnp.where(jnp.broadcast_to(part, (128, 128)) < col, 1.0, 0.0)
    before = jnp.sum(total, axis=1, keepdims=True)
    place = (SPAN + iota((128, 1), 0)).astype(F32) - before
    return col, place


def turn(high, low, tab_ref):
    rows = high.shape[0]
    parts = []
    for which, value in enumerate((high, low)):
        hot = jnp.where(iota((rows, 32), 1).astype(F32) == value, 1.0, 0.0).astype(BF)
        got = mm(hot, tab_ref[which])
        parts.append(got[:, :256] + got[:, 256:512] + got[:, 512:])
    (ch, sh), (cl, sl) = [(p[:, :128], p[:, 128:]) for p in parts]
    first = lax.rem(iota((1, 128), 1), 64) < 32
    sine = sh * cl + ch * sl
    return ch * cl - sh * sl, jnp.where(first, -sine, sine)


def rotated(part, cosine, sine):
    first = lax.rem(iota((1, 128), 1), 64) < 32
    other = jnp.where(first, pltpu.roll(part, 96, 1), pltpu.roll(part, 32, 1))
    return part * cosine + other * sine


def split_place(place):
    high = jnp.floor(place * (1.0 / 32.0))
    return high, place - 32.0 * high


def slots_kernel(tok_ref, owner_row, owner_col, ids_ref, slots_ref, info_ref, wide, stage, place_all):
    pages = BLK // PAGE
    same = owner_col[...] == owner_row[...]
    earlier = iota((pages, pages), 0) < iota((pages, pages), 1)
    rank = jnp.sum(jnp.where(same & earlier, 1.0, 0.0), axis=0, keepdims=True)
    target = owner_row[...].astype(F32) * CAP + rank
    hot = jnp.where(iota((N_TOK * CAP, pages), 0).astype(F32) == target, 1.0, 0.0).astype(BF)
    for k in range(D // 128):
        wide[k] = tok_ref[:, k * 128 : k * 128 + 128].astype(F32)
    for t in range(PAGE):
        part = jnp.concatenate([wide[k, pl.ds(t, pages, stride=PAGE), :] for k in range(D // 128)], axis=1)
        placed = mm(hot, part.astype(BF))
        for k in range(D // 128):
            stage[k % 4, pl.ds(k // 4 * 4 + t, N_TOK * CAP, stride=8), :] = placed[:, k * 128 : k * 128 + 128]
    for k in range(4):
        slots_ref[:, k * 128 : k * 128 + 128] = stage[k].astype(BF)
    for k in range(BLK // 128):
        _, place = ids_and_places(ids_ref, BLK * REACH // 128 + k)
        place_all[pl.ds(k * 128, 128), :] = jnp.broadcast_to(place, (128, 128))
    lane = iota((pages, 128), 1)
    info = jnp.zeros((N_TOK, 128), F32)
    for r in range(CAP):
        packed = jnp.zeros((pages, 128), F32)
        for t in range(PAGE):
            high, low = split_place(place_all[pl.ds(t, pages, stride=PAGE), :])
            packed = jnp.where(lane == r * 8 + t * 2, high, packed)
            packed = jnp.where(lane == r * 8 + t * 2 + 1, low, packed)
        pick = jnp.where((iota((N_TOK, pages), 0) * CAP + r).astype(F32) == target, 1.0, 0.0)
        info = info + mm(pick.astype(BF), packed.astype(BF))
    info_ref[...] = info[:, None, :]


def build_slots(tokens, owner_row, owner_col, ids_row):
    return pl.pallas_call(
        slots_kernel,
        out_shape=(
            jax.ShapeDtypeStruct((N_TOK * CAP * 8, 512), BF),
            jax.ShapeDtypeStruct((N_TOK, 1, 128), F32),
        ),
        in_specs=[VMEM] * 4,
        out_specs=[VMEM] * 2,
        scratch_shapes=[
            pltpu.VMEM((D // 128, BLK, 128), F32),
            pltpu.VMEM((4, N_TOK * CAP * 8, 128), F32),
            pltpu.VMEM((BLK, 128), F32),
        ],
    )(tokens, owner_row, owner_col, ids_row)


PAIRS = 2


def main_kernel(bounds, window_ref, wqkv_hbm, wo_hbm, ids_ref, gain_ref, tab_ref, slots_hbm, info_ref,
                out_ref, cache_ref,
                tok, wqkv, wo, keys, values, heads, scores, mixed, slots, stage, sems):
    copies = [
        pltpu.make_async_copy(window_ref, tok.at[pl.ds(0, WIN)], sems.at[0]),
        pltpu.make_async_copy(wqkv_hbm, wqkv, sems.at[1]),
        pltpu.make_async_copy(slots_hbm, slots, sems.at[2]),
        pltpu.make_async_copy(wo_hbm, wo, sems.at[3]),
    ]
    for copy in copies:
        copy.start()
    gain = gain_ref[...]
    first_row = bounds[6]
    copies[0].wait()
    copies[1].wait()
    for t in range(3):
        here = pl.ds(REACH * BLK + t * 128, 128)
        normed = layer_norm(tok[here, :].astype(F32), gain).astype(BF)
        _, place = ids_and_places(ids_ref, REACH * 3 + t)
        cosine, sine = turn(*split_place(place), tab_ref)
        part = mm(normed, wqkv[:, :D])
        for pair in range(H // 2):
            turned = rotated(part[:, pair * 128 : pair * 128 + 128], cosine, sine).astype(BF) * BF(0.125)
            left = iota((128, 128), 1) < 64
            none = jnp.zeros((128, 128), BF)
            heads[t, pair, :128, :] = jnp.where(left, turned, none)
            heads[t, pair, 128:, :] = jnp.where(left, none, turned)
    low = bounds[0]
    count = (bounds[5] + 2 - low) // 2

    def project(i, _):
        chunk = low + i * 2
        start = pl.multiple_of(chunk * 128, 128)
        here = pl.ds(start, 256)
        local = start + iota((256, 1), 0)
        real = (local < WIN) & (local + first_row >= REACH * BLK) & (local + first_row < N_TOK * 4 * BLK + REACH * BLK)
        normed = jnp.where(real, layer_norm(tok[here, :].astype(F32), gain), 0.0).astype(BF)
        place = jnp.concatenate([ids_and_places(ids_ref, chunk)[1], ids_and_places(ids_ref, chunk + 1)[1]], axis=0)
        cosine, sine = turn(*split_place(place), tab_ref)
        for part in range(2):
            got = mm(normed, wqkv[:, D + part * 512 : D + part * 512 + 512])
            for k in range(4):
                lanes = pl.ds(part * 512 + k * 128, 128)
                keys[here, lanes] = rotated(got[:, k * 128 : k * 128 + 128], cosine, sine).astype(BF)
        values[here, :] = mm(normed, wqkv[:, 2 * D :]).astype(BF)
        return 0

    lax.fori_loop(0, count, project, 0)
    for t in range(3):
        id_col = column(ids_ref[:, pl.ds(SPAN + REACH * BLK + t * 128, 128)].astype(F32))
        id_col = jnp.concatenate([id_col, id_col], axis=0)
        begin = bounds[t]
        steps = (bounds[3 + t] - begin + 1) // 2

        def pairs(group, _):
            lane0 = [pl.multiple_of((group * PAIRS + j) * 128, 128) for j in range(PAIRS)]

            def score(i, peaks):
                start = pl.multiple_of((begin + i * 2) * 128, 128)
                id_row = ids_ref[:, pl.ds(pl.multiple_of(start + SPAN, 128), 256)].astype(F32)
                allowed = id_col == id_row
                new = []
                for j in range(PAIRS):
                    got = lax.dot_general(
                        heads[t, group * PAIRS + j], keys[pl.ds(start, 256), pl.ds(lane0[j], 128)],
                        (((1,), (1,)), ((), ())), preferred_element_type=F32)
                    got = jnp.where(allowed, got, NEG_FILL)
                    scores[j, i] = got
                    new.append(jnp.maximum(peaks[j], jnp.maximum(got[:, :128], got[:, 128:])))
                return tuple(new)

            peaks = lax.fori_loop(0, steps, score, (jnp.full((256, 128), NEG_FILL, F32),) * PAIRS)
            peaks = [jnp.max(p, axis=1, keepdims=True) for p in peaks]

            def mix(i, carry):
                start = pl.multiple_of((begin + i * 2) * 128, 128)
                new = []
                for j in range(PAIRS):
                    total, acc = carry[j]
                    weight = jnp.exp(scores[j, i] - peaks[j])
                    total = total + weight[:, :128] + weight[:, 128:]
                    acc = acc + mm(weight.astype(BF), values[pl.ds(start, 256), pl.ds(lane0[j], 128)])
                    new.append((total, acc))
                return tuple(new)

            zero = jnp.zeros((256, 128), F32)
            done = lax.fori_loop(0, steps, mix, ((zero, zero),) * PAIRS)
            for j in range(PAIRS):
                total, acc = done[j]
                acc = acc / jnp.sum(total, axis=1, keepdims=True)
                left = iota((128, 128), 1) < 64
                mixed[pl.ds(t * 128, 128), pl.ds(lane0[j], 128)] = jnp.where(left, acc[:128], acc[128:]).astype(BF)
            return 0

        lax.fori_loop(0, H // 2 // PAIRS, pairs, 0)
    copies[3].wait()
    out_ref[...] = mm(mixed[...], wo[...]).astype(BF)
    copies[2].wait()
    for k in range(4):
        stage[k] = slots[:, k * 128 : k * 128 + 128].astype(F32)
    count_slots = N_TOK * CAP
    info = info_ref[:, 0, :].astype(BF)
    lane = iota((count_slots, 128), 1)
    spread = []
    for r in range(CAP):
        pick = iota((count_slots, N_TOK), 0) == iota((count_slots, N_TOK), 1) * CAP + r
        spread.append(mm(jnp.where(pick, 1.0, 0.0).astype(BF), info))

    for t in range(PAGE):
        sides = [stage[k % 4, pl.ds(k // 4 * 4 + t, count_slots, stride=8), :] for k in range(8)]
        normed = layer_norm(jnp.concatenate(sides, axis=1), gain).astype(BF)
        parts = []
        for side in range(2):
            found = jnp.zeros((count_slots, 128), F32)
            for r in range(CAP):
                found = found + jnp.where(lane == r * 8 + t * 2 + side, spread[r], 0.0)
            parts.append(jnp.sum(found, axis=1, keepdims=True))
        cosine, sine = turn(*parts, tab_ref)
        got = mm(normed, wqkv[:, D : 2 * D])
        for k in range(8):
            cache_ref[:, pl.ds(t * 2048 + k * 128, 128)] = rotated(
                got[:, k * 128 : k * 128 + 128], cosine, sine).astype(BF)
        cache_ref[:, pl.ds(t * 2048 + D, D)] = mm(normed, wqkv[:, 2 * D :]).astype(BF)


def main_call(bounds, window, wqkv, wo, ids_row, gain, tables, slots, info):
    return pl.pallas_call(
        main_kernel,
        out_shape=(
            jax.ShapeDtypeStruct((BLK, D), BF),
            jax.ShapeDtypeStruct((N_TOK * CAP, 2 * PAGE * D), BF),
        ),
        in_specs=[SMEM, ANY, ANY, ANY, VMEM, VMEM, VMEM, ANY, VMEM],
        out_specs=[VMEM] * 2,
        scratch_shapes=[
            pltpu.VMEM((WIN + EXTRA, D), BF),
            pltpu.VMEM((D, 3 * D), BF),
            pltpu.VMEM((D, D), BF),
            pltpu.VMEM((WIN + EXTRA, D), BF),
            pltpu.VMEM((WIN + EXTRA, D), BF),
            pltpu.VMEM((3, H // 2, 256, 128), BF),
            pltpu.VMEM((PAIRS, 11, 256, 256), F32),
            pltpu.VMEM((BLK, D), BF),
            pltpu.VMEM((N_TOK * CAP * 8, 512), BF),
            pltpu.VMEM((4, N_TOK * CAP * 8, 128), F32),
            pltpu.SemaphoreType.DMA((4,)),
        ],
        compiler_params=pltpu.CompilerParams(vmem_limit_bytes=60 * 1024 * 1024),
    )(bounds, window, wqkv, wo, ids_row, gain, tables, slots, info)


def remote(src, dst, ssem, rsem, tok, grp):
    return pltpu.make_async_remote_copy(src_ref=src, dst_ref=dst, send_sem=ssem, recv_sem=rsem,
                                        device_id=(tok, grp), device_id_type=MESH)

def comm_kernel(tok_ref, win_ref, wout_ref, slots_ref, place_ref,
                wqkv_ref, wo_ref, window_ref, slots_out, place_out,
                xs, xr, zs, zr, ys, yr, hs, hr, bs, br, ts, tr, us, ur, ns, nr, ps, pr, loc):
    do = {"weights": True, "tokens": True, "pages": True}
    a = lax.axis_index("tok"); x = lax.axis_index("grp")
    c = lax.rem(a, 2); z = lax.rem(a // 2, NZ); y = a // (2 * NZ)
    tok_of = lambda yy, zz, cc: (yy * NZ + zz) * 2 + cc
    ring = lambda v, d, n: lax.rem(v + d + n, n)
    sib = a + 1 - 2 * c
    n_tok = NY * NZ * 2
    barrier = pltpu.get_barrier_semaphore()

    def greet(j, _):
        pl.semaphore_signal(barrier, inc=1, device_id=(lax.rem(a + j, n_tok), x), device_id_type=MESH)
        return 0
    lax.fori_loop(1, n_tok, greet, 0)
    for d in range(1, 4):
        pl.semaphore_signal(barrier, inc=1, device_id=(a, lax.rem(x + d, 4)), device_id_type=MESH)
    pl.semaphore_wait(barrier, n_tok - 1 + 3)

    weights = ((win_ref, wqkv_ref, 768), (wout_ref, wo_ref, 256))
    rows_of = lambda aa: pl.ds(pl.multiple_of(aa * 16, 16), 16)
    half_rows = lambda aa, h: pl.ds(pl.multiple_of(aa * 16 + 8 * h, 8), 8)

    xp, xm, xo = ring(x, 1, 4), ring(x, -1, 4), ring(x, 2, 4)
    widx = lambda xx, at: 3 + xx - at
    if do["weights"]:
        for w, (sh, full, cols) in enumerate(weights):
            place = full.at[rows_of(a), pl.ds(pl.multiple_of(x * cols, 128), cols)]
            pltpu.make_async_copy(sh, place, loc.at[w]).start()
            for d in range(1, 4):
                remote(sh, place, xs.at[w, d], xr.at[w, d], a, ring(x, d, 4)).start()
    if do["tokens"]:
        pltpu.make_async_copy(tok_ref, window_ref.at[3], loc.at[2]).start()
        remote(tok_ref, window_ref.at[widx(x, xp)], ts.at[0], tr.at[0], a, xp).start()
        remote(tok_ref, window_ref.at[widx(x, xm)], ts.at[1], tr.at[1], a, xm).start()
    if do["pages"]:
        mine = pl.ds(a * 3, 3)
        pltpu.make_async_copy(slots_ref.at[mine], slots_out.at[mine], loc.at[3]).start()
        pltpu.make_async_copy(place_ref.at[a], place_out.at[a], loc.at[4]).start()

        def send_pages(lo, hi):
            def one(j, _):
                peer = lax.rem(a + lax.rem(j * 27, n_tok), n_tok)
                remote(slots_ref.at[pl.ds(peer * 3, 3)], slots_out.at[mine], ps.at[0], pr.at[0], peer, x).start()
                remote(place_ref.at[peer], place_out.at[a], ps.at[1], pr.at[1], peer, x).start()
                return 0
            lax.fori_loop(lo, hi, one, 0)
    else:
        send_pages = lambda lo, hi: None
    send_pages(1, 16)

    if do["weights"]:
        def got(w, aa, sem):
            full = weights[w][1]
            remote(full.at[rows_of(aa)], full.at[rows_of(aa)], sem, sem, a, xp).wait_recv()
        def got_half(w, aa, h, sem):
            full = weights[w][1]
            remote(full.at[half_rows(aa, h)], full.at[half_rows(aa, h)], sem, sem, a, xp).wait_recv()
        def y_send(w, zz):
            full = weights[w][1]
            blk = full.at[rows_of(tok_of(y, zz, c))]
            remote(blk, blk, ys.at[w, 0, zz], yr.at[w, 0, zz], tok_of(ring(y, 1, NY), z, c), x).start()
            remote(blk, blk, ys.at[w, 1, zz], yr.at[w, 1, zz], tok_of(ring(y, -1, NY), z, c), x).start()
        def sib_send(w, yy, zz):
            full = weights[w][1]
            blk = full.at[rows_of(tok_of(yy, zz, c))]
            remote(blk, blk, bs.at[w, yy, zz], br.at[w, yy, zz], sib, x).start()
        def z_send(w, zz, dirn):
            full = weights[w][1]
            blk = full.at[rows_of(tok_of(y, zz, c))]
            remote(blk, blk, zs.at[w, dirn, zz], zr.at[w, zz], tok_of(y, ring(z, 1 - 2 * dirn, NZ), c), x).start()
        def spread(w, zz):
            y_send(w, zz)
            sib_send(w, y, zz)
        def y_relay(w, zz):
            full = weights[w][1]
            ym, yp = ring(y, -1, NY), ring(y, 1, NY)
            got(w, tok_of(ym, zz, c), yr.at[w, 0, zz])
            h = full.at[half_rows(tok_of(ym, zz, c), 0)]
            remote(h, h, hs.at[w, 0, zz], hr.at[w, 0, zz], tok_of(yp, z, c), x).start()
            sib_send(w, ym, zz)
            got(w, tok_of(yp, zz, c), yr.at[w, 1, zz])
            h = full.at[half_rows(tok_of(yp, zz, c), 1)]
            remote(h, h, hs.at[w, 1, zz], hr.at[w, 1, zz], tok_of(ym, z, c), x).start()
            sib_send(w, yp, zz)
        def y_last(w, zz):
            yo = ring(y, 2, NY)
            got_half(w, tok_of(yo, zz, c), 0, hr.at[w, 0, zz])
            got_half(w, tok_of(yo, zz, c), 1, hr.at[w, 1, zz])
            sib_send(w, yo, zz)
        W = (0, 1)
        for w in W:
            sh, full, cols = weights[w]
            place = full.at[rows_of(a), pl.ds(pl.multiple_of(x * cols, 128), cols)]
            pltpu.make_async_copy(sh, place, loc.at[w]).wait()
            for d in range(1, 4):
                src = ring(x, -d, 4)
                p = full.at[rows_of(a), pl.ds(pl.multiple_of(src * cols, 128), cols)]
                remote(sh, p, xs.at[w, d], xr.at[w, d], a, xp).wait()
        for w in W:
            z_send(w, z, 0); z_send(w, z, 1)
        for w in W:
            spread(w, z)
    send_pages(16, 24)
    if do["weights"]:
        def zstep(k, _):
            zp, zm = ring(z, -k, NZ), lax.rem(z + k, NZ)
            for w in W:
                got(w, tok_of(y, zp, c), zr.at[w, zp])
                @pl.when(k < 4)
                def _(): z_send(w, zp, 0)
            @pl.when(k < 4)
            def _():
                for w in W:
                    got(w, tok_of(y, zm, c), zr.at[w, zm])
                    @pl.when(k < 3)
                    def _(): z_send(w, zm, 1)
            for w in W:
                spread(w, zp)
            @pl.when(k < 4)
            def _():
                for w in W: spread(w, zm)
            send_pages(24 + (k - 1) * 10, 24 + k * 10)
            return 0
        lax.fori_loop(1, 5, zstep, 0)
    else:
        send_pages(24, 64)
    if do["tokens"]:
        hb = BLK // 2
        top, bot = pl.ds(0, hb), pl.ds(hb, hb)
        wfull = lambda xx, s: remote(tok_ref, window_ref.at[widx(xx, x)], tr.at[s], tr.at[s], a, xp)
        wfull(xm, 0).wait_recv()
        remote(window_ref.at[widx(xm, x), top], window_ref.at[widx(xm, xp), top], us.at[0], ur.at[0], a, xp).start()
        wfull(xp, 1).wait_recv()
        remote(window_ref.at[widx(xp, x), bot], window_ref.at[widx(xp, xm), bot], us.at[1], ur.at[1], a, xm).start()
        def cross(xx, k):
            @pl.when((xx > x) & (a < n_tok - 1))
            def _(): remote(window_ref.at[widx(xx, x)], window_ref.at[xx - x - 1], ns.at[0, k], nr.at[0, k], a + 1, x).start()
            @pl.when((xx < x) & (a > 0))
            def _(): remote(window_ref.at[widx(xx, x)], window_ref.at[xx - x + 7], ns.at[1, k], nr.at[1, k], a - 1, x).start()
        cross(xm, 0); cross(xp, 1)
    def order(i):
        return lax.rem(z + jnp.where(lax.rem(i, 2) == 1, NZ - (i + 1) // 2, i // 2), NZ)
    if do["weights"]:
        def relay(i, _):
            for w in W: y_relay(w, order(i))
            return 0
        lax.fori_loop(0, 4, relay, 0)
    if do["tokens"]:
        wh = lambda s, part: remote(window_ref.at[widx(xo, x), part], window_ref.at[widx(xo, x), part], ur.at[s], ur.at[s], a, xp)
        wh(0, top).wait_recv(); wh(1, bot).wait_recv()
        cross(xo, 2)
    if do["weights"]:
        lax.fori_loop(4, NZ, relay, 0)
        def last(i, _):
            for w in W: y_last(w, order(i))
            return 0
        lax.fori_loop(0, NZ, last, 0)
        def sibs(i, _):
            yy, zz = i // NZ, lax.rem(i, NZ)
            for w in W:
                full = weights[w][1]
                mine_blk = full.at[rows_of(tok_of(yy, zz, c))]
                blk = full.at[rows_of(tok_of(yy, zz, 1 - c))]
                remote(blk, blk, bs.at[w, yy, zz], br.at[w, yy, zz], sib, x).wait_recv()
                remote(mine_blk, mine_blk, bs.at[w, yy, zz], br.at[w, yy, zz], sib, x).wait_send()
            return 0
        lax.fori_loop(0, NY * NZ, sibs, 0)
        def drain(zz, _):
            for w in W:
                full = weights[w][1]
                blk = full.at[rows_of(a)]; h = full.at[half_rows(a, 0)]
                for d in range(2):
                    remote(blk, blk, ys.at[w, d, zz], yr.at[w, d, zz], sib, x).wait_send()
                    remote(h, h, hs.at[w, d, zz], hr.at[w, d, zz], sib, x).wait_send()
            return 0
        lax.fori_loop(0, NZ, drain, 0)
        def zdrain(k, _):
            for w in W:
                full = weights[w][1]
                blk = full.at[rows_of(a)]
                zz = ring(z, -k, NZ)
                remote(blk, blk, zs.at[w, 0, zz], zr.at[w, zz], sib, x).wait_send()
                @pl.when(k < 3)
                def _():
                    zq = lax.rem(z + k, NZ)
                    remote(blk, blk, zs.at[w, 1, zq], zr.at[w, zq], sib, x).wait_send()
            return 0
        lax.fori_loop(0, 4, zdrain, 0)
    if do["tokens"]:
        blk = window_ref.at[3]
        hv = window_ref.at[3, top]
        for d in range(2):
            remote(blk, blk, ts.at[d], tr.at[d], a, xp).wait_send()
            remote(hv, hv, us.at[d], ur.at[d], a, xp).wait_send()
        pltpu.make_async_copy(tok_ref, window_ref.at[3], loc.at[2]).wait()
        for k, xx in enumerate((xm, xp, xo)):
            up, down = (xx > x), (xx < x)
            @pl.when(up & (a < n_tok - 1))
            def _(): remote(blk, blk, ns.at[0, k], nr.at[0, k], a, xp).wait_send()
            @pl.when(down & (a > 0))
            def _(): remote(blk, blk, ns.at[1, k], nr.at[1, k], a, xp).wait_send()
            @pl.when(up & (a > 0))
            def _():
                d = window_ref.at[xx - x - 1]
                remote(d, d, ns.at[0, k], nr.at[0, k], a, xp).wait_recv()
            @pl.when(down & (a < n_tok - 1))
            def _():
                d = window_ref.at[xx - x + 7]
                remote(d, d, ns.at[1, k], nr.at[1, k], a, xp).wait_recv()
    if do["pages"]:
        pltpu.make_async_copy(slots_ref.at[mine], slots_out.at[mine], loc.at[3]).wait()
        pltpu.make_async_copy(place_ref.at[a], place_out.at[a], loc.at[4]).wait()
        rest = pl.ds(0, (n_tok - 1) * 3)
        prest = pl.ds(0, n_tok - 1)
        cp = remote(slots_ref.at[rest], slots_out.at[rest], ps.at[0], pr.at[0], a, xp); cp.wait()
        cp = remote(place_ref.at[prest], place_out.at[prest], ps.at[1], pr.at[1], a, xp); cp.wait()

def comm(tokens, w_in, w_out, slots, place):
    D = pltpu.SemaphoreType.DMA
    return pl.pallas_call(
        comm_kernel,
        out_shape=(jax.ShapeDtypeStruct((1024, 3072), BF), jax.ShapeDtypeStruct((1024, 1024), BF),
                   jax.ShapeDtypeStruct((7, tokens.shape[0], 1024), BF),
                   jax.ShapeDtypeStruct(slots.shape, BF), jax.ShapeDtypeStruct(place.shape, place.dtype)),
        in_specs=[ANY] * 5, out_specs=[ANY] * 5,
        scratch_shapes=[D((2, 4)), D((2, 4)), D((2, 2, NZ)), D((2, NZ)), D((2, 2, NZ)), D((2, 2, NZ)),
                        D((2, 2, NZ)), D((2, 2, NZ)), D((2, NY, NZ)), D((2, NY, NZ)), D((2,)), D((2,)), D((2,)), D((2,)),
                        D((2, 3)), D((2, 3)), D((2,)), D((2,)), D((5,))],
        compiler_params=pltpu.CompilerParams(collective_id=0, has_side_effects=True),
    )(tokens, w_in, w_out, slots, place)


def per_device(tokens, norm_gain, input_weight, output_weight, segment_ids, page_owner, tables):
    device = lax.axis_index("tok") * 4 + lax.axis_index("grp")
    first_row = device * BLK
    ahead = SPAN + REACH * BLK
    padded = jnp.concatenate([
        jnp.full((ahead,), -1, jnp.int32), segment_ids, jnp.full((REACH * BLK + EXTRA,), TOP, jnp.int32)])
    ids = lax.dynamic_slice_in_dim(padded, first_row, SPAN + WIN + EXTRA, 0)
    reach = ids[SPAN : SPAN + WIN]
    own = reach[REACH * BLK : (REACH + 1) * BLK].reshape(3, 128)
    begin = jnp.sum((reach[None, :] < own[:, :1]).astype(jnp.int32), axis=1) // 128
    end = (jnp.sum((reach[None, :] <= own[:, 127:]).astype(jnp.int32), axis=1) + 127) // 128
    bounds = jnp.concatenate([begin, end, first_row[None], first_row[None]])
    ids_row = ids[None, :]
    slots, info = build_slots(tokens, page_owner.reshape(1, -1), page_owner, ids_row)
    wqkv, wo, window, slots, info = comm(tokens, input_weight, output_weight, slots.reshape(N_TOK * CAP, 8, 512), info)
    return main_call(bounds, window.reshape(WIN, D), wqkv, wo, ids_row, norm_gain[None, :], tables,
                     slots.reshape(N_TOK * CAP * 8, 512), info)


def solution(mesh):
    placed = (
        P(("tok", "grp"), None),
        P(),
        P("tok", "grp"),
        P("tok", "grp"),
        P(),
        P(("tok", "grp"), None),
        P(),
    )
    tables = rope_tables()
    step = jax.shard_map(
        per_device,
        mesh=mesh,
        in_specs=placed,
        out_specs=(P(("tok", "grp"), None), P(("tok", "grp"), None)),
        check_vma=False,
    )
    return lambda *args: step(*args, jnp.asarray(tables))
```

```python
import functools

import jax
import jax.numpy as jnp
import ml_dtypes
import numpy as np
from jax import lax
from jax.experimental import pallas as pl
from jax.experimental.pallas import tpu as pltpu
from jax.sharding import PartitionSpec as P

D = 1024
H = 16
SPAN = 1024
PAGE = 4
CAP = 3
BLK = 384
REACH = 3
WIN = (2 * REACH + 1) * BLK
EXTRA = 256
NEG_FILL = -1e30
ROPE_BASE = 160000.0
EPSILON = 1e-5
N_TOK = 64
NY, NZ = 4, 8
ROWS = 16
TOP = 1 << 30

MESH = pl.DeviceIdType.MESH
ANY = pl.BlockSpec(memory_space=pl.ANY)
VMEM = pl.BlockSpec(memory_space=pltpu.VMEM)
SMEM = pl.BlockSpec(memory_space=pltpu.SMEM)
BF, F32 = jnp.bfloat16, jnp.float32


def rope_tables():
    freq = 1.0 / ROPE_BASE ** (np.arange(32) * 2.0 / 64)
    lanes = np.tile(freq, 4)
    out = []
    for step in (32.0, 1.0):
        angle = step * np.arange(32)[:, None] * lanes[None, :]
        rest = np.concatenate([np.cos(angle), np.sin(angle)], axis=1)
        terms = []
        for _ in range(3):
            term = rest.astype(ml_dtypes.bfloat16)
            terms.append(term)
            rest = rest - term.astype(np.float64)
        out.append(np.concatenate(terms, axis=1))
    return np.stack(out)


def mm(left, right):
    return jnp.dot(left, right, preferred_element_type=F32)


def layer_norm(values, gain):
    center = jnp.mean(values, axis=-1, keepdims=True)
    moved = values - center
    spread = jnp.mean(jnp.square(moved), axis=-1, keepdims=True)
    return moved * lax.rsqrt(spread + EPSILON) * gain


def iota(shape, axis):
    return lax.broadcasted_iota(jnp.int32, shape, axis)


def column(row):
    eye = iota((128, 128), 0) == iota((128, 128), 1)
    return jnp.sum(jnp.where(eye, jnp.broadcast_to(row, (128, 128)), 0.0), axis=1, keepdims=True)


def ids_and_places(ids_ref, chunk):
    base = pl.multiple_of(chunk * 128, 128)
    own = ids_ref[:, pl.ds(pl.multiple_of(base + SPAN, 128), 128)].astype(F32)
    col = column(own)
    total = jnp.zeros((128, 128), F32)
    for k in range(SPAN // 128 + 1):
        part = ids_ref[:, pl.ds(pl.multiple_of(base + k * 128, 128), 128)].astype(F32)
        total = total + jnp.where(jnp.broadcast_to(part, (128, 128)) < col, 1.0, 0.0)
    before = jnp.sum(total, axis=1, keepdims=True)
    place = (SPAN + iota((128, 1), 0)).astype(F32) - before
    return col, place


def turn(high, low, tab_ref):
    rows = high.shape[0]
    parts = []
    for which, value in enumerate((high, low)):
        hot = jnp.where(iota((rows, 32), 1).astype(F32) == value, 1.0, 0.0).astype(BF)
        got = mm(hot, tab_ref[which])
        parts.append(got[:, :256] + got[:, 256:512] + got[:, 512:])
    (ch, sh), (cl, sl) = [(p[:, :128], p[:, 128:]) for p in parts]
    first = lax.rem(iota((1, 128), 1), 64) < 32
    sine = sh * cl + ch * sl
    return ch * cl - sh * sl, jnp.where(first, -sine, sine)


def rotated(part, cosine, sine):
    first = lax.rem(iota((1, 128), 1), 64) < 32
    other = jnp.where(first, pltpu.roll(part, 96, 1), pltpu.roll(part, 32, 1))
    return part * cosine + other * sine


def split_place(place):
    high = jnp.floor(place * (1.0 / 32.0))
    return high, place - 32.0 * high


def slots_kernel(tok_ref, owner_row, owner_col, ids_ref, slots_ref, info_ref, wide, stage, place_all):
    pages = BLK // PAGE
    same = owner_col[...] == owner_row[...]
    earlier = iota((pages, pages), 0) < iota((pages, pages), 1)
    rank = jnp.sum(jnp.where(same & earlier, 1.0, 0.0), axis=0, keepdims=True)
    target = owner_row[...].astype(F32) * CAP + rank
    hot = jnp.where(iota((N_TOK * CAP, pages), 0).astype(F32) == target, 1.0, 0.0).astype(BF)
    for k in range(D // 128):
        wide[k] = tok_ref[:, k * 128 : k * 128 + 128].astype(F32)
    for t in range(PAGE):
        part = jnp.concatenate([wide[k, pl.ds(t, pages, stride=PAGE), :] for k in range(D // 128)], axis=1)
        placed = mm(hot, part.astype(BF))
        for k in range(D // 128):
            stage[k % 4, pl.ds(k // 4 * 4 + t, N_TOK * CAP, stride=8), :] = placed[:, k * 128 : k * 128 + 128]
    for k in range(4):
        slots_ref[:, k * 128 : k * 128 + 128] = stage[k].astype(BF)
    for k in range(BLK // 128):
        _, place = ids_and_places(ids_ref, BLK * REACH // 128 + k)
        place_all[pl.ds(k * 128, 128), :] = jnp.broadcast_to(place, (128, 128))
    lane = iota((pages, 128), 1)
    info = jnp.zeros((N_TOK, 128), F32)
    for r in range(CAP):
        packed = jnp.zeros((pages, 128), F32)
        for t in range(PAGE):
            high, low = split_place(place_all[pl.ds(t, pages, stride=PAGE), :])
            packed = jnp.where(lane == r * 8 + t * 2, high, packed)
            packed = jnp.where(lane == r * 8 + t * 2 + 1, low, packed)
        pick = jnp.where((iota((N_TOK, pages), 0) * CAP + r).astype(F32) == target, 1.0, 0.0)
        info = info + mm(pick.astype(BF), packed.astype(BF))
    info_ref[...] = info[:, None, :]


def build_slots(tokens, owner_row, owner_col, ids_row):
    return pl.pallas_call(
        slots_kernel,
        out_shape=(
            jax.ShapeDtypeStruct((N_TOK * CAP * 8, 512), BF),
            jax.ShapeDtypeStruct((N_TOK, 1, 128), F32),
        ),
        in_specs=[VMEM] * 4,
        out_specs=[VMEM] * 2,
        scratch_shapes=[
            pltpu.VMEM((D // 128, BLK, 128), F32),
            pltpu.VMEM((4, N_TOK * CAP * 8, 128), F32),
            pltpu.VMEM((BLK, 128), F32),
        ],
    )(tokens, owner_row, owner_col, ids_row)


PAIRS = 2


def main_kernel(bounds, window_ref, wqkv_hbm, wo_hbm, ids_ref, gain_ref, tab_ref, slots_hbm, info_ref,
                out_ref, cache_ref,
                tok, wqkv, wo, keys, values, heads, scores, mixed, slots, stage, sems):
    copies = [
        pltpu.make_async_copy(window_ref, tok.at[pl.ds(0, WIN)], sems.at[0]),
        pltpu.make_async_copy(wqkv_hbm, wqkv, sems.at[1]),
        pltpu.make_async_copy(slots_hbm, slots, sems.at[2]),
        pltpu.make_async_copy(wo_hbm, wo, sems.at[3]),
    ]
    for copy in copies:
        copy.start()
    gain = gain_ref[...]
    first_row = bounds[6]
    copies[0].wait()
    copies[1].wait()
    for t in range(3):
        here = pl.ds(REACH * BLK + t * 128, 128)
        normed = layer_norm(tok[here, :].astype(F32), gain).astype(BF)
        _, place = ids_and_places(ids_ref, REACH * 3 + t)
        cosine, sine = turn(*split_place(place), tab_ref)
        part = mm(normed, wqkv[:, :D])
        for pair in range(H // 2):
            turned = rotated(part[:, pair * 128 : pair * 128 + 128], cosine, sine).astype(BF) * BF(0.125)
            left = iota((128, 128), 1) < 64
            none = jnp.zeros((128, 128), BF)
            heads[t, pair, :128, :] = jnp.where(left, turned, none)
            heads[t, pair, 128:, :] = jnp.where(left, none, turned)
    low = bounds[0]
    count = (bounds[5] + 2 - low) // 2

    def project(i, _):
        chunk = low + i * 2
        start = pl.multiple_of(chunk * 128, 128)
        here = pl.ds(start, 256)
        local = start + iota((256, 1), 0)
        real = (local < WIN) & (local + first_row >= REACH * BLK) & (local + first_row < N_TOK * 4 * BLK + REACH * BLK)
        normed = jnp.where(real, layer_norm(tok[here, :].astype(F32), gain), 0.0).astype(BF)
        place = jnp.concatenate([ids_and_places(ids_ref, chunk)[1], ids_and_places(ids_ref, chunk + 1)[1]], axis=0)
        cosine, sine = turn(*split_place(place), tab_ref)
        for part in range(2):
            got = mm(normed, wqkv[:, D + part * 512 : D + part * 512 + 512])
            for k in range(4):
                lanes = pl.ds(part * 512 + k * 128, 128)
                keys[here, lanes] = rotated(got[:, k * 128 : k * 128 + 128], cosine, sine).astype(BF)
        values[here, :] = mm(normed, wqkv[:, 2 * D :]).astype(BF)
        return 0

    lax.fori_loop(0, count, project, 0)
    for t in range(3):
        id_col = column(ids_ref[:, pl.ds(SPAN + REACH * BLK + t * 128, 128)].astype(F32))
        id_col = jnp.concatenate([id_col, id_col], axis=0)
        begin = bounds[t]
        steps = (bounds[3 + t] - begin + 1) // 2

        def pairs(group, _):
            lane0 = [pl.multiple_of((group * PAIRS + j) * 128, 128) for j in range(PAIRS)]

            def score(i, peaks):
                start = pl.multiple_of((begin + i * 2) * 128, 128)
                id_row = ids_ref[:, pl.ds(pl.multiple_of(start + SPAN, 128), 256)].astype(F32)
                allowed = id_col == id_row
                new = []
                for j in range(PAIRS):
                    got = lax.dot_general(
                        heads[t, group * PAIRS + j], keys[pl.ds(start, 256), pl.ds(lane0[j], 128)],
                        (((1,), (1,)), ((), ())), preferred_element_type=F32)
                    got = jnp.where(allowed, got, NEG_FILL)
                    scores[j, i] = got
                    new.append(jnp.maximum(peaks[j], jnp.maximum(got[:, :128], got[:, 128:])))
                return tuple(new)

            peaks = lax.fori_loop(0, steps, score, (jnp.full((256, 128), NEG_FILL, F32),) * PAIRS)
            peaks = [jnp.max(p, axis=1, keepdims=True) for p in peaks]

            def mix(i, carry):
                start = pl.multiple_of((begin + i * 2) * 128, 128)
                new = []
                for j in range(PAIRS):
                    total, acc = carry[j]
                    weight = jnp.exp(scores[j, i] - peaks[j])
                    total = total + weight[:, :128] + weight[:, 128:]
                    acc = acc + mm(weight.astype(BF), values[pl.ds(start, 256), pl.ds(lane0[j], 128)])
                    new.append((total, acc))
                return tuple(new)

            zero = jnp.zeros((256, 128), F32)
            done = lax.fori_loop(0, steps, mix, ((zero, zero),) * PAIRS)
            for j in range(PAIRS):
                total, acc = done[j]
                acc = acc / jnp.sum(total, axis=1, keepdims=True)
                left = iota((128, 128), 1) < 64
                mixed[pl.ds(t * 128, 128), pl.ds(lane0[j], 128)] = jnp.where(left, acc[:128], acc[128:]).astype(BF)
            return 0

        lax.fori_loop(0, H // 2 // PAIRS, pairs, 0)
    copies[3].wait()
    out_ref[...] = mm(mixed[...], wo[...]).astype(BF)
    copies[2].wait()
    for k in range(4):
        stage[k] = slots[:, k * 128 : k * 128 + 128].astype(F32)
    count_slots = N_TOK * CAP
    info = info_ref[:, 0, :].astype(BF)
    lane = iota((count_slots, 128), 1)
    spread = []
    for r in range(CAP):
        pick = iota((count_slots, N_TOK), 0) == iota((count_slots, N_TOK), 1) * CAP + r
        spread.append(mm(jnp.where(pick, 1.0, 0.0).astype(BF), info))

    for t in range(PAGE):
        sides = [stage[k % 4, pl.ds(k // 4 * 4 + t, count_slots, stride=8), :] for k in range(8)]
        normed = layer_norm(jnp.concatenate(sides, axis=1), gain).astype(BF)
        parts = []
        for side in range(2):
            found = jnp.zeros((count_slots, 128), F32)
            for r in range(CAP):
                found = found + jnp.where(lane == r * 8 + t * 2 + side, spread[r], 0.0)
            parts.append(jnp.sum(found, axis=1, keepdims=True))
        cosine, sine = turn(*parts, tab_ref)
        got = mm(normed, wqkv[:, D : 2 * D])
        for k in range(8):
            cache_ref[:, pl.ds(t * 2048 + k * 128, 128)] = rotated(
                got[:, k * 128 : k * 128 + 128], cosine, sine).astype(BF)
        cache_ref[:, pl.ds(t * 2048 + D, D)] = mm(normed, wqkv[:, 2 * D :]).astype(BF)


def main_call(bounds, window, wqkv, wo, ids_row, gain, tables, slots, info):
    return pl.pallas_call(
        main_kernel,
        out_shape=(
            jax.ShapeDtypeStruct((BLK, D), BF),
            jax.ShapeDtypeStruct((N_TOK * CAP, 2 * PAGE * D), BF),
        ),
        in_specs=[SMEM, ANY, ANY, ANY, VMEM, VMEM, VMEM, ANY, VMEM],
        out_specs=[VMEM] * 2,
        scratch_shapes=[
            pltpu.VMEM((WIN + EXTRA, D), BF),
            pltpu.VMEM((D, 3 * D), BF),
            pltpu.VMEM((D, D), BF),
            pltpu.VMEM((WIN + EXTRA, D), BF),
            pltpu.VMEM((WIN + EXTRA, D), BF),
            pltpu.VMEM((3, H // 2, 256, 128), BF),
            pltpu.VMEM((PAIRS, 11, 256, 256), F32),
            pltpu.VMEM((BLK, D), BF),
            pltpu.VMEM((N_TOK * CAP * 8, 512), BF),
            pltpu.VMEM((4, N_TOK * CAP * 8, 128), F32),
            pltpu.SemaphoreType.DMA((4,)),
        ],
        compiler_params=pltpu.CompilerParams(vmem_limit_bytes=60 * 1024 * 1024),
    )(bounds, window, wqkv, wo, ids_row, gain, tables, slots, info)


def remote(src, dst, ssem, rsem, tok, grp):
    return pltpu.make_async_remote_copy(src_ref=src, dst_ref=dst, send_sem=ssem, recv_sem=rsem,
                                        device_id=(tok, grp), device_id_type=MESH)

def comm_kernel(tok_ref, win_ref, wout_ref, slots_ref, place_ref,
                wqkv_ref, wo_ref, window_ref, slots_out, place_out, outer_ref,
                xs, xr, zs, zr, ys, yr, hs, hr, bs, br, ts, tr, us, ur, ns, nr, os, fs, fr, ps, pr, loc):
    do = {"weights": True, "tokens": True, "pages": True}
    a = lax.axis_index("tok"); x = lax.axis_index("grp")
    c = lax.rem(a, 2); z = lax.rem(a // 2, NZ); y = a // (2 * NZ)
    tok_of = lambda yy, zz, cc: (yy * NZ + zz) * 2 + cc
    ring = lambda v, d, n: lax.rem(v + d + n, n)
    sib = a + 1 - 2 * c
    n_tok = NY * NZ * 2
    barrier = pltpu.get_barrier_semaphore()

    def greet(j, _):
        pl.semaphore_signal(barrier, inc=1, device_id=(lax.rem(a + j, n_tok), x), device_id_type=MESH)
        return 0
    lax.fori_loop(1, n_tok, greet, 0)
    for d in range(1, 4):
        pl.semaphore_signal(barrier, inc=1, device_id=(a, lax.rem(x + d, 4)), device_id_type=MESH)
    pl.semaphore_wait(barrier, n_tok - 1 + 3)

    full = (wqkv_ref, wo_ref)
    shard = (win_ref, wout_ref)
    width = (768, 256)
    W = (0, 1)
    rows_of = lambda aa: pl.ds(pl.multiple_of(aa * 16, 16), 16)
    half_rows = lambda aa, h: pl.ds(pl.multiple_of(aa * 16 + 8 * h, 8), 8)
    block = lambda w, aa: full[w].at[rows_of(aa)]
    half = lambda w, aa, h: full[w].at[half_rows(aa, h)]
    piece = lambda w, aa, xx: full[w].at[rows_of(aa), pl.ds(pl.multiple_of(xx * width[w], 128), width[w])]
    xp, xm, xo = ring(x, 1, 4), ring(x, -1, 4), ring(x, 2, 4)
    widx = lambda xx, at: 3 + xx - at
    taken = lambda ref, sem: remote(ref, ref, sem, sem, a, xp).wait_recv()
    left = lambda ref, sem: remote(ref, ref, sem, sem, a, xp).wait_send()

    def z_send(w, zz, dirn, src=None):
        here = piece(w, tok_of(y, zz, c), x)
        remote(here if src is None else src, here, zs.at[w, dirn, zz], zr.at[w, zz],
               tok_of(y, ring(z, 1 - 2 * dirn, NZ), c), x).start()
    def x_send(w, zz, src=None):
        here = piece(w, tok_of(y, zz, c), x)
        for d in range(1, 4):
            remote(here if src is None else src, here, xs.at[w, d - 1, zz], xr.at[w, d - 1, zz], a, ring(x, d, 4)).start()
    def sib_send(w, yy, zz):
        blk = block(w, tok_of(yy, zz, c))
        remote(blk, blk, bs.at[w, yy, zz], br.at[w, yy, zz], sib, x).start()
    def join(w, zz):
        for d in range(1, 4):
            taken(piece(w, tok_of(y, zz, c), ring(x, -d, 4)), xr.at[w, d - 1, zz])
        blk = block(w, tok_of(y, zz, c))
        remote(blk, blk, ys.at[w, 0, zz], yr.at[w, 0, zz], tok_of(ring(y, 1, NY), z, c), x).start()
        remote(blk, blk, ys.at[w, 1, zz], yr.at[w, 1, zz], tok_of(ring(y, -1, NY), z, c), x).start()
        sib_send(w, y, zz)
    def y_relay(w, zz):
        ym, yp = ring(y, -1, NY), ring(y, 1, NY)
        taken(block(w, tok_of(ym, zz, c)), yr.at[w, 0, zz])
        h = half(w, tok_of(ym, zz, c), 0)
        remote(h, h, hs.at[w, 0, zz], hr.at[w, 0, zz], tok_of(yp, z, c), x).start()
        sib_send(w, ym, zz)
        taken(block(w, tok_of(yp, zz, c)), yr.at[w, 1, zz])
        h = half(w, tok_of(yp, zz, c), 1)
        remote(h, h, hs.at[w, 1, zz], hr.at[w, 1, zz], tok_of(ym, z, c), x).start()
        sib_send(w, yp, zz)
    def y_last(w, zz):
        yo = ring(y, 2, NY)
        taken(half(w, tok_of(yo, zz, c), 0), hr.at[w, 0, zz])
        taken(half(w, tok_of(yo, zz, c), 1), hr.at[w, 1, zz])
        sib_send(w, yo, zz)
    def z_step(k):
        zp, zm = ring(z, -k, NZ), lax.rem(z + k, NZ)
        for w in W:
            taken(piece(w, tok_of(y, zp, c), x), zr.at[w, zp])
            if k < 4: z_send(w, zp, 0)
        if k < 4:
            for w in W:
                taken(piece(w, tok_of(y, zm, c), x), zr.at[w, zm])
                if k < 3: z_send(w, zm, 1)
        for w in W:
            x_send(w, zp)
            if k < 4: x_send(w, zm)
    def joins(k):
        for w in W: join(w, ring(z, -k, NZ))
        if 0 < k < 4:
            for w in W: join(w, lax.rem(z + k, NZ))

    sgn = 1 - 2 * c
    u = jnp.where(c == 0, x, 3 - x)
    at_u = lambda v: jnp.where(c == 0, v, 3 - v)
    far = a - sgn
    linked = (far >= 0) & (far < n_tok)
    fidx = lambda uu, at: (at_u(uu) - at_u(at)) - 1 + 8 * c
    hb = BLK // 2
    top, bot = pl.ds(0, hb), pl.ds(hb, hb)
    def cross(xx, k):
        @pl.when((xx - x) * sgn > 0)
        def _():
            remote(window_ref.at[widx(xx, x)], window_ref.at[xx - x - 1 + 8 * c], ns.at[k], nr.at[k], sib, x).start()
    def outer_on():
        @pl.when(linked & (u >= 1))
        def _():
            taken(outer_ref, os.at[1])
            remote(outer_ref, window_ref.at[fidx(u, u - 1)], fs.at[0], fr.at[0], a, at_u(u - 1)).start()
        @pl.when(linked & (u == 3))
        def _():
            remote(outer_ref, window_ref.at[fidx(3, 0)], fs.at[1], fr.at[1], a, at_u(0)).start()
    def outer_relay():
        @pl.when(linked & (u <= 2))
        def _():
            taken(window_ref.at[fidx(u + 1, u)], fr.at[0])
        @pl.when(linked & (u >= 1) & (u <= 2))
        def _():
            remote(window_ref.at[fidx(u + 1, u)], window_ref.at[fidx(u + 1, u - 1)], fs.at[2], fr.at[2], a, at_u(u - 1)).start()
    def ring_relay():
        taken(window_ref.at[widx(xm, x)], tr.at[0])
        remote(window_ref.at[widx(xm, x), top], window_ref.at[widx(xm, xp), top], us.at[0], ur.at[0], a, xp).start()
        taken(window_ref.at[widx(xp, x)], tr.at[1])
        remote(window_ref.at[widx(xp, x), bot], window_ref.at[widx(xp, xm), bot], us.at[1], ur.at[1], a, xm).start()
        cross(xm, 0); cross(xp, 1)

    mine = pl.ds(a * 3, 3)
    def send_pages(lo, hi):
        if not do["pages"]: return
        def one(j, _):
            peer = lax.rem(a + lax.rem(j * 27, n_tok), n_tok)
            remote(slots_ref.at[pl.ds(peer * 3, 3)], slots_out.at[mine], ps.at[0], pr.at[0], peer, x).start()
            remote(place_ref.at[peer], place_out.at[a], ps.at[1], pr.at[1], peer, x).start()
            return 0
        lax.fori_loop(lo, hi, one, 0)

    if do["weights"]:
        for w in W:
            pltpu.make_async_copy(shard[w], piece(w, a, x), loc.at[w]).start()
            z_send(w, z, 0, shard[w]); z_send(w, z, 1, shard[w])
            x_send(w, z, shard[w])
    if do["tokens"]:
        pltpu.make_async_copy(tok_ref, window_ref.at[3], loc.at[2]).start()
        @pl.when(linked & (u <= 2))
        def _(): remote(tok_ref, outer_ref, os.at[0], os.at[1], far, x).start()
        remote(tok_ref, window_ref.at[widx(x, xp)], ts.at[0], tr.at[0], a, xp).start()
        remote(tok_ref, window_ref.at[widx(x, xm)], ts.at[1], tr.at[1], a, xm).start()
    if do["pages"]:
        pltpu.make_async_copy(slots_ref.at[mine], slots_out.at[mine], loc.at[3]).start()
        pltpu.make_async_copy(place_ref.at[a], place_out.at[a], loc.at[4]).start()
    send_pages(1, 12)
    if do["weights"]:
        for w in W: pltpu.make_async_copy(shard[w], piece(w, a, x), loc.at[w]).wait()
        z_step(1); joins(0)
    send_pages(12, 20)
    if do["weights"]:
        z_step(2); joins(1)
    send_pages(20, 28)
    if do["weights"]: z_step(3)
    if do["tokens"]: outer_on()
    send_pages(28, 36)
    if do["weights"]:
        joins(2); z_step(4)
    send_pages(36, 64)
    if do["tokens"]: ring_relay()
    if do["weights"]:
        joins(3)
    order = lambda i: lax.rem(z + jnp.where(lax.rem(i, 2) == 1, NZ - (i + 1) // 2, i // 2), NZ)
    def relays(lo, hi):
        def relay(i, _):
            for w in W: y_relay(w, order(i))
            return 0
        lax.fori_loop(lo, hi, relay, 0)
    if do["weights"]:
        relays(0, 2)
        joins(4)
    if do["tokens"]: outer_relay()
    if do["weights"]: relays(2, 5)
    if do["tokens"]:
        taken(window_ref.at[widx(xo, x), top], ur.at[0])
        taken(window_ref.at[widx(xo, x), bot], ur.at[1])
        cross(xo, 2)
    if do["weights"]:
        relays(5, NZ)
        def last(i, _):
            for w in W: y_last(w, order(i))
            return 0
        lax.fori_loop(0, NZ, last, 0)
        def sibs(i, _):
            yy, zz = i // NZ, lax.rem(i, NZ)
            for w in W:
                taken(block(w, tok_of(yy, zz, 1 - c)), br.at[w, yy, zz])
                left(block(w, tok_of(yy, zz, c)), bs.at[w, yy, zz])
            return 0
        lax.fori_loop(0, NY * NZ, sibs, 0)
        def drain(zz, _):
            for w in W:
                for d in range(2):
                    left(block(w, a), ys.at[w, d, zz])
                    left(half(w, a, 0), hs.at[w, d, zz])
                for d in range(3):
                    left(piece(w, a, x), xs.at[w, d, zz])
            return 0
        lax.fori_loop(0, NZ, drain, 0)
        for k in range(4):
            for w in W:
                left(piece(w, a, x), zs.at[w, 0, ring(z, -k, NZ)])
                if k < 3: left(piece(w, a, x), zs.at[w, 1, lax.rem(z + k, NZ)])
    if do["tokens"]:
        blk = window_ref.at[3]
        hv = window_ref.at[3, top]
        for d in range(2):
            left(blk, ts.at[d]); left(hv, us.at[d])
        pltpu.make_async_copy(tok_ref, window_ref.at[3], loc.at[2]).wait()
        for k, xx in enumerate((xm, xp, xo)):
            @pl.when((xx - x) * sgn > 0)
            def _(): left(blk, ns.at[k])
            @pl.when((xx - x) * sgn < 0)
            def _(): taken(window_ref.at[xx - x + 7 - 8 * c], nr.at[k])
        @pl.when(linked & (u <= 2))
        def _(): left(blk, os.at[0])
        @pl.when(linked & (u >= 1))
        def _(): left(blk, fs.at[0])
        @pl.when(linked & (u == 3))
        def _(): left(blk, fs.at[1])
        @pl.when(linked & (u >= 1) & (u <= 2))
        def _(): left(blk, fs.at[2])
        @pl.when(linked & (u == 0))
        def _(): taken(window_ref.at[fidx(3, 0)], fr.at[1])
        @pl.when(linked & (u <= 1))
        def _(): taken(window_ref.at[fidx(u + 2, u)], fr.at[2])
    if do["pages"]:
        pltpu.make_async_copy(slots_ref.at[mine], slots_out.at[mine], loc.at[3]).wait()
        pltpu.make_async_copy(place_ref.at[a], place_out.at[a], loc.at[4]).wait()
        rest = pl.ds(0, (n_tok - 1) * 3)
        prest = pl.ds(0, n_tok - 1)
        remote(slots_ref.at[rest], slots_out.at[rest], ps.at[0], pr.at[0], a, xp).wait()
        remote(place_ref.at[prest], place_out.at[prest], ps.at[1], pr.at[1], a, xp).wait()

def comm(tokens, w_in, w_out, slots, place):
    D_ = pltpu.SemaphoreType.DMA
    return pl.pallas_call(
        comm_kernel,
        out_shape=(jax.ShapeDtypeStruct((1024, 3072), BF), jax.ShapeDtypeStruct((1024, 1024), BF),
                   jax.ShapeDtypeStruct((7, tokens.shape[0], 1024), BF),
                   jax.ShapeDtypeStruct(slots.shape, BF), jax.ShapeDtypeStruct(place.shape, place.dtype),
                   jax.ShapeDtypeStruct(tokens.shape, BF)),
        in_specs=[ANY] * 5, out_specs=[ANY] * 6,
        scratch_shapes=[D_((2, 3, NZ)), D_((2, 3, NZ)), D_((2, 2, NZ)), D_((2, NZ)), D_((2, 2, NZ)), D_((2, 2, NZ)),
                        D_((2, 2, NZ)), D_((2, 2, NZ)), D_((2, NY, NZ)), D_((2, NY, NZ)), D_((2,)), D_((2,)), D_((2,)), D_((2,)),
                        D_((3,)), D_((3,)), D_((2,)), D_((3,)), D_((3,)), D_((2,)), D_((2,)), D_((5,))],
        compiler_params=pltpu.CompilerParams(collective_id=0, has_side_effects=True),
    )(tokens, w_in, w_out, slots, place)[:5]


def per_device(tokens, norm_gain, input_weight, output_weight, segment_ids, page_owner, tables):
    device = lax.axis_index("tok") * 4 + lax.axis_index("grp")
    first_row = device * BLK
    ahead = SPAN + REACH * BLK
    padded = jnp.concatenate([
        jnp.full((ahead,), -1, jnp.int32), segment_ids, jnp.full((REACH * BLK + EXTRA,), TOP, jnp.int32)])
    ids = lax.dynamic_slice_in_dim(padded, first_row, SPAN + WIN + EXTRA, 0)
    reach = ids[SPAN : SPAN + WIN]
    own = reach[REACH * BLK : (REACH + 1) * BLK].reshape(3, 128)
    begin = jnp.sum((reach[None, :] < own[:, :1]).astype(jnp.int32), axis=1) // 128
    end = (jnp.sum((reach[None, :] <= own[:, 127:]).astype(jnp.int32), axis=1) + 127) // 128
    bounds = jnp.concatenate([begin, end, first_row[None], first_row[None]])
    ids_row = ids[None, :]
    slots, info = build_slots(tokens, page_owner.reshape(1, -1), page_owner, ids_row)
    wqkv, wo, window, slots, info = comm(tokens, input_weight, output_weight, slots.reshape(N_TOK * CAP, 8, 512), info)
    return main_call(bounds, window.reshape(WIN, D), wqkv, wo, ids_row, norm_gain[None, :], tables,
                     slots.reshape(N_TOK * CAP * 8, 512), info)


def solution(mesh):
    placed = (
        P(("tok", "grp"), None),
        P(),
        P("tok", "grp"),
        P("tok", "grp"),
        P(),
        P(("tok", "grp"), None),
        P(),
    )
    tables = rope_tables()
    step = jax.shard_map(
        per_device,
        mesh=mesh,
        in_specs=placed,
        out_specs=(P(("tok", "grp"), None), P(("tok", "grp"), None)),
        check_vma=False,
    )
    return lambda *args: step(*args, jnp.asarray(tables))
```

```python
import functools

import jax
import jax.numpy as jnp
import ml_dtypes
import numpy as np
from jax import lax
from jax.experimental import pallas as pl
from jax.experimental.pallas import tpu as pltpu
from jax.sharding import PartitionSpec as P

D = 1024
H = 16
SPAN = 1024
PAGE = 4
CAP = 3
BLK = 384
REACH = 3
WIN = (2 * REACH + 1) * BLK
EXTRA = 256
NEG_FILL = -1e30
ROPE_BASE = 160000.0
EPSILON = 1e-5
N_TOK = 64
NY, NZ = 4, 8
ROWS = 16
TOP = 1 << 30

MESH = pl.DeviceIdType.MESH
ANY = pl.BlockSpec(memory_space=pl.ANY)
VMEM = pl.BlockSpec(memory_space=pltpu.VMEM)
SMEM = pl.BlockSpec(memory_space=pltpu.SMEM)
BF, F32 = jnp.bfloat16, jnp.float32


def rope_tables():
    freq = 1.0 / ROPE_BASE ** (np.arange(32) * 2.0 / 64)
    lanes = np.tile(freq, 4)
    out = []
    for step in (32.0, 1.0):
        angle = step * np.arange(32)[:, None] * lanes[None, :]
        rest = np.concatenate([np.cos(angle), np.sin(angle)], axis=1)
        terms = []
        for _ in range(3):
            term = rest.astype(ml_dtypes.bfloat16)
            terms.append(term)
            rest = rest - term.astype(np.float64)
        out.append(np.concatenate(terms, axis=1))
    return np.stack(out)


def mm(left, right):
    return jnp.dot(left, right, preferred_element_type=F32)


def layer_norm(values, gain):
    center = jnp.mean(values, axis=-1, keepdims=True)
    moved = values - center
    spread = jnp.mean(jnp.square(moved), axis=-1, keepdims=True)
    return moved * lax.rsqrt(spread + EPSILON) * gain


def iota(shape, axis):
    return lax.broadcasted_iota(jnp.int32, shape, axis)


def column(row):
    eye = iota((128, 128), 0) == iota((128, 128), 1)
    return jnp.sum(jnp.where(eye, jnp.broadcast_to(row, (128, 128)), 0.0), axis=1, keepdims=True)


def ids_and_places(ids_ref, chunk):
    base = pl.multiple_of(chunk * 128, 128)
    own = ids_ref[:, pl.ds(pl.multiple_of(base + SPAN, 128), 128)].astype(F32)
    col = column(own)
    total = jnp.zeros((128, 128), F32)
    for k in range(SPAN // 128 + 1):
        part = ids_ref[:, pl.ds(pl.multiple_of(base + k * 128, 128), 128)].astype(F32)
        total = total + jnp.where(jnp.broadcast_to(part, (128, 128)) < col, 1.0, 0.0)
    before = jnp.sum(total, axis=1, keepdims=True)
    place = (SPAN + iota((128, 1), 0)).astype(F32) - before
    return col, place


def turn(high, low, tab_ref):
    rows = high.shape[0]
    parts = []
    for which, value in enumerate((high, low)):
        hot = jnp.where(iota((rows, 32), 1).astype(F32) == value, 1.0, 0.0).astype(BF)
        got = mm(hot, tab_ref[which])
        parts.append(got[:, :256] + got[:, 256:512] + got[:, 512:])
    (ch, sh), (cl, sl) = [(p[:, :128], p[:, 128:]) for p in parts]
    first = lax.rem(iota((1, 128), 1), 64) < 32
    sine = sh * cl + ch * sl
    return ch * cl - sh * sl, jnp.where(first, -sine, sine)


def rotated(part, cosine, sine):
    first = lax.rem(iota((1, 128), 1), 64) < 32
    other = jnp.where(first, pltpu.roll(part, 96, 1), pltpu.roll(part, 32, 1))
    return part * cosine + other * sine


def split_place(place):
    high = jnp.floor(place * (1.0 / 32.0))
    return high, place - 32.0 * high


def slots_kernel(tok_ref, owner_row, ids_ref, slots_ref, info_ref, wide, stage, place_all):
    pages = BLK // PAGE
    owner = owner_row[...].astype(F32)
    eye = iota((pages, pages), 0) == iota((pages, pages), 1)
    owner_col = jnp.sum(jnp.where(eye, jnp.broadcast_to(owner, (pages, pages)), 0.0), axis=1, keepdims=True)
    same = owner_col == owner
    earlier = iota((pages, pages), 0) < iota((pages, pages), 1)
    rank = jnp.sum(jnp.where(same & earlier, 1.0, 0.0), axis=0, keepdims=True)
    target = owner * CAP + rank
    hot = jnp.where(iota((N_TOK * CAP, pages), 0).astype(F32) == target, 1.0, 0.0).astype(BF)
    for k in range(D // 128):
        wide[k] = tok_ref[:, k * 128 : k * 128 + 128].astype(F32)
    for t in range(PAGE):
        part = jnp.concatenate([wide[k, pl.ds(t, pages, stride=PAGE), :] for k in range(D // 128)], axis=1)
        placed = mm(hot, part.astype(BF))
        for k in range(D // 128):
            stage[k % 4, pl.ds(k // 4 * 4 + t, N_TOK * CAP, stride=8), :] = placed[:, k * 128 : k * 128 + 128]
    for k in range(4):
        slots_ref[:, k * 128 : k * 128 + 128] = stage[k].astype(BF)
    for k in range(BLK // 128):
        _, place = ids_and_places(ids_ref, BLK * REACH // 128 + k)
        place_all[pl.ds(k * 128, 128), :] = jnp.broadcast_to(place, (128, 128))
    lane = iota((pages, 128), 1)
    info = jnp.zeros((N_TOK, 128), F32)
    for r in range(CAP):
        packed = jnp.zeros((pages, 128), F32)
        for t in range(PAGE):
            high, low = split_place(place_all[pl.ds(t, pages, stride=PAGE), :])
            packed = jnp.where(lane == r * 8 + t * 2, high, packed)
            packed = jnp.where(lane == r * 8 + t * 2 + 1, low, packed)
        pick = jnp.where((iota((N_TOK, pages), 0) * CAP + r).astype(F32) == target, 1.0, 0.0)
        info = info + mm(pick.astype(BF), packed.astype(BF))
    info_ref[...] = info[:, None, :]


def build_slots(tokens, owner_row, ids_row):
    return pl.pallas_call(
        slots_kernel,
        out_shape=(
            jax.ShapeDtypeStruct((N_TOK * CAP * 8, 512), BF),
            jax.ShapeDtypeStruct((N_TOK, 1, 128), F32),
        ),
        in_specs=[VMEM] * 3,
        out_specs=[VMEM] * 2,
        scratch_shapes=[
            pltpu.VMEM((D // 128, BLK, 128), F32),
            pltpu.VMEM((4, N_TOK * CAP * 8, 128), F32),
            pltpu.VMEM((BLK, 128), F32),
        ],
    )(tokens, owner_row, ids_row)


PAIRS = 2


def main_kernel(bounds, window_ref, wqkv_hbm, wo_hbm, ids_ref, gain_ref, tab_ref, slots_hbm, info_ref,
                out_ref, cache_ref,
                tok, wqkv, wo, keys, values, marks, heads, scores, mixed, slots, stage, sems):
    own = pl.ds(REACH * BLK, BLK)
    before, after = pl.ds(0, REACH * BLK), pl.ds((REACH + 1) * BLK, REACH * BLK)
    copies = [
        pltpu.make_async_copy(window_ref.at[own], tok.at[own], sems.at[0]),
        pltpu.make_async_copy(wqkv_hbm.at[:, :D], wqkv.at[:, :D], sems.at[1]),
        pltpu.make_async_copy(wqkv_hbm.at[:, D:], wqkv.at[:, D:], sems.at[4]),
        pltpu.make_async_copy(window_ref.at[before], tok.at[before], sems.at[5]),
        pltpu.make_async_copy(window_ref.at[after], tok.at[after], sems.at[6]),
        pltpu.make_async_copy(slots_hbm, slots, sems.at[2]),
        pltpu.make_async_copy(wo_hbm, wo, sems.at[3]),
    ]
    for copy in copies:
        copy.start()
    gain = gain_ref[...]
    first_row = bounds[6]
    copies[0].wait()
    copies[1].wait()
    for t in range(3):
        here = pl.ds(REACH * BLK + t * 128, 128)
        normed = layer_norm(tok[here, :].astype(F32), gain).astype(BF)
        _, place = ids_and_places(ids_ref, REACH * 3 + t)
        cosine, sine = turn(*split_place(place), tab_ref)
        part = mm(normed, wqkv[:, :D])
        for pair in range(H // 2):
            turned = rotated(part[:, pair * 128 : pair * 128 + 128], cosine, sine)
            turned = turned.T.astype(BF).astype(F32) * 0.125
            upper = iota((128, 128), 0) < 64
            heads[t, pair, :, :128] = jnp.where(upper, turned, 0.0).astype(BF)
            heads[t, pair, :, 128:] = jnp.where(upper, 0.0, turned).astype(BF)
    for k in range(2, 5):
        copies[k].wait()
    low = bounds[0]
    count = (bounds[5] + 2 - low) // 2

    def project(i, _):
        chunk = low + i * 2
        start = pl.multiple_of(chunk * 128, 128)
        here = pl.ds(start, 256)
        local = start + iota((256, 1), 0)
        real = (local < WIN) & (local + first_row >= REACH * BLK) & (local + first_row < N_TOK * 4 * BLK + REACH * BLK)
        normed = jnp.where(real, layer_norm(tok[here, :].astype(F32), gain), 0.0).astype(BF)
        pieces = [ids_and_places(ids_ref, chunk + k) for k in range(2)]
        place = jnp.concatenate([p[1] for p in pieces], axis=0)
        for k in range(2):
            marks[pl.ds(pl.multiple_of(start + k * 128, 128), 128), :] = jnp.broadcast_to(pieces[k][0], (128, 128))
        cosine, sine = turn(*split_place(place), tab_ref)
        for part in range(2):
            got = mm(normed, wqkv[:, D + part * 512 : D + part * 512 + 512])
            for k in range(4):
                lanes = pl.ds(part * 512 + k * 128, 128)
                keys[here, lanes] = rotated(got[:, k * 128 : k * 128 + 128], cosine, sine).astype(BF)
        for part in range(2):
            got = mm(normed, wqkv[:, 2 * D + part * 512 : 2 * D + part * 512 + 512])
            for k in range(4):
                lane = part * 512 + k * 128
                values[pl.ds(lane, 128), here] = got[:, k * 128 : k * 128 + 128].T.astype(BF)
        return 0

    lax.fori_loop(0, count, project, 0)
    fold = lambda op, value: op(value.reshape(32, 8, 128), axis=0)
    for t in range(3):
        id_row = ids_ref[:, pl.ds(SPAN + REACH * BLK + t * 128, 128)].astype(F32)
        begin = bounds[t]
        steps = (bounds[3 + t] - begin + 1) // 2

        def pairs(group, _):
            lane0 = [pl.multiple_of((group * PAIRS + j) * 128, 128) for j in range(PAIRS)]

            def score(i, peaks):
                start = pl.multiple_of((begin + i * 2) * 128, 128)
                allowed = marks[pl.ds(start, 256), :] == id_row
                new = []
                for j in range(PAIRS):
                    got = mm(keys[pl.ds(start, 256), pl.ds(lane0[j], 128)], heads[t, group * PAIRS + j])
                    for side in range(2):
                        half = jnp.where(allowed, got[:, side * 128 : side * 128 + 128], NEG_FILL)
                        scores[j, i, side] = half
                        new.append(jnp.maximum(peaks[2 * j + side], fold(jnp.max, half)))
                return tuple(new)

            peaks = lax.fori_loop(0, steps, score, (jnp.full((8, 128), NEG_FILL, F32),) * (2 * PAIRS))
            peaks = [jnp.max(p, axis=0, keepdims=True) for p in peaks]

            def mix(i, carry):
                start = pl.multiple_of((begin + i * 2) * 128, 128)
                totals, accs = [], []
                for j in range(PAIRS):
                    both = []
                    for side in range(2):
                        weight = jnp.exp(scores[j, i, side] - peaks[2 * j + side])
                        totals.append(carry[2 * j + side] + fold(jnp.sum, weight))
                        both.append(weight.astype(BF))
                    accs.append(carry[2 * PAIRS + j] + mm(
                        values[pl.ds(lane0[j], 128), pl.ds(start, 256)], jnp.concatenate(both, axis=1)))
                return tuple(totals + accs)

            done = lax.fori_loop(
                0, steps, mix, (jnp.zeros((8, 128), F32),) * (2 * PAIRS) + (jnp.zeros((128, 256), F32),) * PAIRS)
            for j in range(PAIRS):
                total = [jnp.sum(done[2 * j + side], axis=0, keepdims=True) for side in range(2)]
                acc = done[2 * PAIRS + j]
                upper = iota((128, 128), 0) < 64
                picked = jnp.where(upper, acc[:, :128] / total[0], acc[:, 128:] / total[1])
                mixed[pl.ds(t * 128, 128), pl.ds(lane0[j], 128)] = picked.T.astype(BF)
            return 0

        lax.fori_loop(0, H // 2 // PAIRS, pairs, 0)
    copies[6].wait()
    out_ref[...] = mm(mixed[...], wo[...]).astype(BF)
    copies[5].wait()
    for k in range(4):
        stage[k] = slots[:, k * 128 : k * 128 + 128].astype(F32)
    count_slots = N_TOK * CAP
    info = info_ref[:, 0, :].astype(BF)
    lane = iota((count_slots, 128), 1)
    spread = []
    for r in range(CAP):
        pick = iota((count_slots, N_TOK), 0) == iota((count_slots, N_TOK), 1) * CAP + r
        spread.append(mm(jnp.where(pick, 1.0, 0.0).astype(BF), info))

    for t in range(PAGE):
        sides = [stage[k % 4, pl.ds(k // 4 * 4 + t, count_slots, stride=8), :] for k in range(8)]
        normed = layer_norm(jnp.concatenate(sides, axis=1), gain).astype(BF)
        parts = []
        for side in range(2):
            found = jnp.zeros((count_slots, 128), F32)
            for r in range(CAP):
                found = found + jnp.where(lane == r * 8 + t * 2 + side, spread[r], 0.0)
            parts.append(jnp.sum(found, axis=1, keepdims=True))
        cosine, sine = turn(*parts, tab_ref)
        got = mm(normed, wqkv[:, D : 2 * D])
        for k in range(8):
            cache_ref[:, pl.ds(t * 2048 + k * 128, 128)] = rotated(
                got[:, k * 128 : k * 128 + 128], cosine, sine).astype(BF)
        cache_ref[:, pl.ds(t * 2048 + D, D)] = mm(normed, wqkv[:, 2 * D :]).astype(BF)


def main_call(bounds, window, wqkv, wo, ids_row, gain, tables, slots, info):
    return pl.pallas_call(
        main_kernel,
        out_shape=(
            jax.ShapeDtypeStruct((BLK, D), BF),
            jax.ShapeDtypeStruct((N_TOK * CAP, 2 * PAGE * D), BF),
        ),
        in_specs=[SMEM, ANY, ANY, ANY, VMEM, VMEM, VMEM, ANY, VMEM],
        out_specs=[VMEM] * 2,
        scratch_shapes=[
            pltpu.VMEM((WIN + EXTRA, D), BF),
            pltpu.VMEM((D, 3 * D), BF),
            pltpu.VMEM((D, D), BF),
            pltpu.VMEM((WIN + EXTRA, D), BF),
            pltpu.VMEM((D, WIN + EXTRA), BF),
            pltpu.VMEM((WIN + EXTRA, 128), F32),
            pltpu.VMEM((3, H // 2, 128, 256), BF),
            pltpu.VMEM((PAIRS, 11, 2, 256, 128), F32),
            pltpu.VMEM((BLK, D), BF),
            pltpu.VMEM((N_TOK * CAP * 8, 512), BF),
            pltpu.VMEM((4, N_TOK * CAP * 8, 128), F32),
            pltpu.SemaphoreType.DMA((7,)),
        ],
        compiler_params=pltpu.CompilerParams(vmem_limit_bytes=60 * 1024 * 1024),
    )(bounds, window, wqkv, wo, ids_row, gain, tables, slots, info)


def remote(src, dst, ssem, rsem, tok, grp):
    return pltpu.make_async_remote_copy(src_ref=src, dst_ref=dst, send_sem=ssem, recv_sem=rsem,
                                        device_id=(tok, grp), device_id_type=MESH)

CUT = (1, 12, 20, 28, 36, 64)


def comm_kernel(tok_ref, win_ref, wout_ref, slots_ref, place_ref,
                wqkv_ref, wo_ref, window_ref, slots_out, place_out, outer_ref,
                xs, xr, zs, zr, ys, yr, hs, hr, bs, br, ts, tr, us, ur, ns, nr, os, fs, fr, ps, pr, loc):
    do = {"weights": True, "tokens": True, "pages": True}
    a = lax.axis_index("tok"); x = lax.axis_index("grp")
    c = lax.rem(a, 2); z = lax.rem(a // 2, NZ); y = a // (2 * NZ)
    tok_of = lambda yy, zz, cc: (yy * NZ + zz) * 2 + cc
    ring = lambda v, d, n: lax.rem(v + d + n, n)
    sib = a + 1 - 2 * c
    n_tok = NY * NZ * 2
    barrier = pltpu.get_barrier_semaphore()

    def greet(j, _):
        pl.semaphore_signal(barrier, inc=1, device_id=(lax.rem(a + j, n_tok), x), device_id_type=MESH)
        return 0
    lax.fori_loop(1, n_tok, greet, 0)
    for d in range(1, 4):
        pl.semaphore_signal(barrier, inc=1, device_id=(a, lax.rem(x + d, 4)), device_id_type=MESH)
    pl.semaphore_wait(barrier, n_tok - 1 + 3)

    full = (wqkv_ref, wo_ref)
    shard = (win_ref, wout_ref)
    width = (768, 256)
    W = (0, 1)
    rows_of = lambda aa: pl.ds(pl.multiple_of(aa * 16, 16), 16)
    half_rows = lambda aa, h: pl.ds(pl.multiple_of(aa * 16 + 8 * h, 8), 8)
    block = lambda w, aa: full[w].at[rows_of(aa)]
    half = lambda w, aa, h: full[w].at[half_rows(aa, h)]
    piece = lambda w, aa, xx: full[w].at[rows_of(aa), pl.ds(pl.multiple_of(xx * width[w], 128), width[w])]
    xp, xm, xo = ring(x, 1, 4), ring(x, -1, 4), ring(x, 2, 4)
    widx = lambda xx, at: 3 + xx - at
    taken = lambda ref, sem: remote(ref, ref, sem, sem, a, xp).wait_recv()
    left = lambda ref, sem: remote(ref, ref, sem, sem, a, xp).wait_send()

    def z_send(w, zz, dirn, src=None):
        here = piece(w, tok_of(y, zz, c), x)
        remote(here if src is None else src, here, zs.at[w, dirn, zz], zr.at[w, zz],
               tok_of(y, ring(z, 1 - 2 * dirn, NZ), c), x).start()
    def x_send(w, zz, src=None):
        here = piece(w, tok_of(y, zz, c), x)
        for d in range(1, 4):
            remote(here if src is None else src, here, xs.at[w, d - 1, zz], xr.at[w, d - 1, zz], a, ring(x, d, 4)).start()
    def sib_send(w, yy, zz):
        blk = block(w, tok_of(yy, zz, c))
        remote(blk, blk, bs.at[w, yy, zz], br.at[w, yy, zz], sib, x).start()
    def join(w, zz):
        for d in range(1, 4):
            taken(piece(w, tok_of(y, zz, c), ring(x, -d, 4)), xr.at[w, d - 1, zz])
        blk = block(w, tok_of(y, zz, c))
        remote(blk, blk, ys.at[w, 0, zz], yr.at[w, 0, zz], tok_of(ring(y, 1, NY), z, c), x).start()
        remote(blk, blk, ys.at[w, 1, zz], yr.at[w, 1, zz], tok_of(ring(y, -1, NY), z, c), x).start()
        sib_send(w, y, zz)
    def y_relay(w, zz):
        ym, yp = ring(y, -1, NY), ring(y, 1, NY)
        taken(block(w, tok_of(ym, zz, c)), yr.at[w, 0, zz])
        h = half(w, tok_of(ym, zz, c), 0)
        remote(h, h, hs.at[w, 0, zz], hr.at[w, 0, zz], tok_of(yp, z, c), x).start()
        sib_send(w, ym, zz)
        taken(block(w, tok_of(yp, zz, c)), yr.at[w, 1, zz])
        h = half(w, tok_of(yp, zz, c), 1)
        remote(h, h, hs.at[w, 1, zz], hr.at[w, 1, zz], tok_of(ym, z, c), x).start()
        sib_send(w, yp, zz)
    def y_last(w, zz):
        yo = ring(y, 2, NY)
        taken(half(w, tok_of(yo, zz, c), 0), hr.at[w, 0, zz])
        taken(half(w, tok_of(yo, zz, c), 1), hr.at[w, 1, zz])
        sib_send(w, yo, zz)
    def z_step(k):
        zp, zm = ring(z, -k, NZ), lax.rem(z + k, NZ)
        for w in W:
            taken(piece(w, tok_of(y, zp, c), x), zr.at[w, zp])
            if k < 4: z_send(w, zp, 0)
        if k < 4:
            for w in W:
                taken(piece(w, tok_of(y, zm, c), x), zr.at[w, zm])
                if k < 3: z_send(w, zm, 1)
        for w in W:
            x_send(w, zp)
            if k < 4: x_send(w, zm)
    def joins(k):
        for w in W: join(w, ring(z, -k, NZ))
        if 0 < k < 4:
            for w in W: join(w, lax.rem(z + k, NZ))

    sgn = 1 - 2 * c
    u = jnp.where(c == 0, x, 3 - x)
    at_u = lambda v: jnp.where(c == 0, v, 3 - v)
    far = a - sgn
    linked = (far >= 0) & (far < n_tok)
    fidx = lambda uu, at: (at_u(uu) - at_u(at)) - 1 + 8 * c
    hb = BLK // 2
    top, bot = pl.ds(0, hb), pl.ds(hb, hb)
    def cross(xx, k):
        @pl.when((xx - x) * sgn > 0)
        def _():
            remote(window_ref.at[widx(xx, x)], window_ref.at[xx - x - 1 + 8 * c], ns.at[k], nr.at[k], sib, x).start()
    def outer_on():
        @pl.when(linked & (u >= 1))
        def _():
            taken(outer_ref, os.at[1])
            remote(outer_ref, window_ref.at[fidx(u, u - 1)], fs.at[0], fr.at[0], a, at_u(u - 1)).start()
        @pl.when(linked & (u == 3))
        def _():
            remote(outer_ref, window_ref.at[fidx(3, 0)], fs.at[1], fr.at[1], a, at_u(0)).start()
    def outer_relay():
        @pl.when(linked & (u <= 2))
        def _():
            taken(window_ref.at[fidx(u + 1, u)], fr.at[0])
        @pl.when(linked & (u >= 1) & (u <= 2))
        def _():
            remote(window_ref.at[fidx(u + 1, u)], window_ref.at[fidx(u + 1, u - 1)], fs.at[2], fr.at[2], a, at_u(u - 1)).start()
    def ring_relay():
        taken(window_ref.at[widx(xm, x)], tr.at[0])
        remote(window_ref.at[widx(xm, x), top], window_ref.at[widx(xm, xp), top], us.at[0], ur.at[0], a, xp).start()
        taken(window_ref.at[widx(xp, x)], tr.at[1])
        remote(window_ref.at[widx(xp, x), bot], window_ref.at[widx(xp, xm), bot], us.at[1], ur.at[1], a, xm).start()
        cross(xm, 0); cross(xp, 1)

    mine = pl.ds(a * 3, 3)
    def send_pages(lo, hi):
        if not do["pages"]: return
        def one(j, _):
            peer = lax.rem(a + lax.rem(j * 27, n_tok), n_tok)
            remote(slots_ref.at[pl.ds(peer * 3, 3)], slots_out.at[mine], ps.at[0], pr.at[0], peer, x).start()
            remote(place_ref.at[peer], place_out.at[a], ps.at[1], pr.at[1], peer, x).start()
            return 0
        lax.fori_loop(lo, hi, one, 0)

    if do["weights"]:
        for w in W:
            pltpu.make_async_copy(shard[w], piece(w, a, x), loc.at[w]).start()
            z_send(w, z, 0, shard[w]); z_send(w, z, 1, shard[w])
            x_send(w, z, shard[w])
    if do["tokens"]:
        pltpu.make_async_copy(tok_ref, window_ref.at[3], loc.at[2]).start()
        @pl.when(linked & (u <= 2))
        def _(): remote(tok_ref, outer_ref, os.at[0], os.at[1], far, x).start()
        remote(tok_ref, window_ref.at[widx(x, xp)], ts.at[0], tr.at[0], a, xp).start()
        remote(tok_ref, window_ref.at[widx(x, xm)], ts.at[1], tr.at[1], a, xm).start()
    if do["pages"]:
        pltpu.make_async_copy(slots_ref.at[mine], slots_out.at[mine], loc.at[3]).start()
        pltpu.make_async_copy(place_ref.at[a], place_out.at[a], loc.at[4]).start()
    send_pages(CUT[0], CUT[1])
    if do["weights"]:
        for w in W: pltpu.make_async_copy(shard[w], piece(w, a, x), loc.at[w]).wait()
        z_step(1); joins(0)
    send_pages(CUT[1], CUT[2])
    if do["weights"]:
        z_step(2); joins(1)
    send_pages(CUT[2], CUT[3])
    if do["weights"]: z_step(3)
    if do["tokens"]: outer_on()
    send_pages(CUT[3], CUT[4])
    if do["weights"]:
        joins(2); z_step(4)
    send_pages(CUT[4], CUT[5])
    if do["tokens"]: ring_relay()
    if do["weights"]:
        joins(3)
    order = lambda i: lax.rem(z + jnp.where(lax.rem(i, 2) == 1, NZ - (i + 1) // 2, i // 2), NZ)
    def relays(lo, hi):
        def relay(i, _):
            for w in W: y_relay(w, order(i))
            return 0
        lax.fori_loop(lo, hi, relay, 0)
    if do["weights"]:
        relays(0, 2)
        joins(4)
    if do["tokens"]: outer_relay()
    if do["weights"]: relays(2, 5)
    if do["tokens"]:
        taken(window_ref.at[widx(xo, x), top], ur.at[0])
        taken(window_ref.at[widx(xo, x), bot], ur.at[1])
        cross(xo, 2)
    if do["weights"]:
        relays(5, NZ)
        def last(i, _):
            for w in W: y_last(w, order(i))
            return 0
        lax.fori_loop(0, NZ, last, 0)
        def sibs(i, _):
            yy, zz = i // NZ, lax.rem(i, NZ)
            for w in W:
                taken(block(w, tok_of(yy, zz, 1 - c)), br.at[w, yy, zz])
                left(block(w, tok_of(yy, zz, c)), bs.at[w, yy, zz])
            return 0
        lax.fori_loop(0, NY * NZ, sibs, 0)
        def drain(zz, _):
            for w in W:
                for d in range(2):
                    left(block(w, a), ys.at[w, d, zz])
                    left(half(w, a, 0), hs.at[w, d, zz])
                for d in range(3):
                    left(piece(w, a, x), xs.at[w, d, zz])
            return 0
        lax.fori_loop(0, NZ, drain, 0)
        for k in range(4):
            for w in W:
                left(piece(w, a, x), zs.at[w, 0, ring(z, -k, NZ)])
                if k < 3: left(piece(w, a, x), zs.at[w, 1, lax.rem(z + k, NZ)])
    if do["tokens"]:
        blk = window_ref.at[3]
        hv = window_ref.at[3, top]
        for d in range(2):
            left(blk, ts.at[d]); left(hv, us.at[d])
        pltpu.make_async_copy(tok_ref, window_ref.at[3], loc.at[2]).wait()
        for k, xx in enumerate((xm, xp, xo)):
            @pl.when((xx - x) * sgn > 0)
            def _(): left(blk, ns.at[k])
            @pl.when((xx - x) * sgn < 0)
            def _(): taken(window_ref.at[xx - x + 7 - 8 * c], nr.at[k])
        @pl.when(linked & (u <= 2))
        def _(): left(blk, os.at[0])
        @pl.when(linked & (u >= 1))
        def _(): left(blk, fs.at[0])
        @pl.when(linked & (u == 3))
        def _(): left(blk, fs.at[1])
        @pl.when(linked & (u >= 1) & (u <= 2))
        def _(): left(blk, fs.at[2])
        @pl.when(linked & (u == 0))
        def _(): taken(window_ref.at[fidx(3, 0)], fr.at[1])
        @pl.when(linked & (u <= 1))
        def _(): taken(window_ref.at[fidx(u + 2, u)], fr.at[2])
    if do["pages"]:
        pltpu.make_async_copy(slots_ref.at[mine], slots_out.at[mine], loc.at[3]).wait()
        pltpu.make_async_copy(place_ref.at[a], place_out.at[a], loc.at[4]).wait()
        rest = pl.ds(0, (n_tok - 1) * 3)
        prest = pl.ds(0, n_tok - 1)
        remote(slots_ref.at[rest], slots_out.at[rest], ps.at[0], pr.at[0], a, xp).wait()
        remote(place_ref.at[prest], place_out.at[prest], ps.at[1], pr.at[1], a, xp).wait()

def comm(tokens, w_in, w_out, slots, place):
    D_ = pltpu.SemaphoreType.DMA
    return pl.pallas_call(
        comm_kernel,
        out_shape=(jax.ShapeDtypeStruct((1024, 3072), BF), jax.ShapeDtypeStruct((1024, 1024), BF),
                   jax.ShapeDtypeStruct((7, tokens.shape[0], 1024), BF),
                   jax.ShapeDtypeStruct(slots.shape, BF), jax.ShapeDtypeStruct(place.shape, place.dtype),
                   jax.ShapeDtypeStruct(tokens.shape, BF)),
        in_specs=[ANY] * 5, out_specs=[ANY] * 6,
        scratch_shapes=[D_((2, 3, NZ)), D_((2, 3, NZ)), D_((2, 2, NZ)), D_((2, NZ)), D_((2, 2, NZ)), D_((2, 2, NZ)),
                        D_((2, 2, NZ)), D_((2, 2, NZ)), D_((2, NY, NZ)), D_((2, NY, NZ)), D_((2,)), D_((2,)), D_((2,)), D_((2,)),
                        D_((3,)), D_((3,)), D_((2,)), D_((3,)), D_((3,)), D_((2,)), D_((2,)), D_((5,))],
        compiler_params=pltpu.CompilerParams(collective_id=0, has_side_effects=True),
    )(tokens, w_in, w_out, slots, place)[:5]


def per_device(tokens, norm_gain, input_weight, output_weight, segment_ids, page_owner, tables):
    device = lax.axis_index("tok") * 4 + lax.axis_index("grp")
    first_row = device * BLK
    ahead = SPAN + REACH * BLK
    padded = jnp.concatenate([
        jnp.full((ahead,), -1, jnp.int32), segment_ids, jnp.full((REACH * BLK + EXTRA,), TOP, jnp.int32)])
    ids = lax.dynamic_slice_in_dim(padded, first_row, SPAN + WIN + EXTRA, 0)
    reach = ids[SPAN : SPAN + WIN]
    own = reach[REACH * BLK : (REACH + 1) * BLK].reshape(3, 128)
    begin = jnp.sum((reach[None, :] < own[:, :1]).astype(jnp.int32), axis=1) // 128
    end = (jnp.sum((reach[None, :] <= own[:, 127:]).astype(jnp.int32), axis=1) + 127) // 128
    bounds = jnp.concatenate([begin, end, first_row[None], first_row[None]])
    ids_row = ids[None, :]
    slots, info = build_slots(tokens, page_owner.reshape(1, -1), ids_row)
    wqkv, wo, window, slots, info = comm(tokens, input_weight, output_weight, slots.reshape(N_TOK * CAP, 8, 512), info)
    return main_call(bounds, window.reshape(WIN, D), wqkv, wo, ids_row, norm_gain[None, :], tables,
                     slots.reshape(N_TOK * CAP * 8, 512), info)


def solution(mesh):
    placed = (
        P(("tok", "grp"), None),
        P(),
        P("tok", "grp"),
        P("tok", "grp"),
        P(),
        P(("tok", "grp"), None),
        P(),
    )
    tables = rope_tables()
    step = jax.shard_map(
        per_device,
        mesh=mesh,
        in_specs=placed,
        out_specs=(P(("tok", "grp"), None), P(("tok", "grp"), None)),
        check_vma=False,
    )
    return lambda *args: step(*args, jnp.asarray(tables))
```

```python
import functools

import jax
import jax.numpy as jnp
import ml_dtypes
import numpy as np
from jax import lax
from jax.experimental import pallas as pl
from jax.experimental.pallas import tpu as pltpu
from jax.sharding import PartitionSpec as P

D = 1024
H = 16
SPAN = 1024
PAGE = 4
CAP = 3
BLK = 384
REACH = 3
WIN = (2 * REACH + 1) * BLK
EXTRA = 256
NEG_FILL = -1e30
ROPE_BASE = 160000.0
EPSILON = 1e-5
N_TOK = 64
NY, NZ = 4, 8
ROWS = 16
TOP = 1 << 30

MESH = pl.DeviceIdType.MESH
ANY = pl.BlockSpec(memory_space=pl.ANY)
VMEM = pl.BlockSpec(memory_space=pltpu.VMEM)
SMEM = pl.BlockSpec(memory_space=pltpu.SMEM)
BF, F32 = jnp.bfloat16, jnp.float32


def rope_tables():
    freq = 1.0 / ROPE_BASE ** (np.arange(32) * 2.0 / 64)
    lanes = np.tile(freq, 4)
    out = []
    for step in (32.0, 1.0):
        angle = step * np.arange(32)[:, None] * lanes[None, :]
        rest = np.concatenate([np.cos(angle), np.sin(angle)], axis=1)
        terms = []
        for _ in range(3):
            term = rest.astype(ml_dtypes.bfloat16)
            terms.append(term)
            rest = rest - term.astype(np.float64)
        out.append(np.concatenate(terms, axis=1))
    return np.stack(out)


def mm(left, right):
    return jnp.dot(left, right, preferred_element_type=F32)


def layer_norm(values, gain):
    center = jnp.mean(values, axis=-1, keepdims=True)
    moved = values - center
    spread = jnp.mean(jnp.square(moved), axis=-1, keepdims=True)
    return moved * lax.rsqrt(spread + EPSILON) * gain


def iota(shape, axis):
    return lax.broadcasted_iota(jnp.int32, shape, axis)


def column(row):
    eye = iota((128, 128), 0) == iota((128, 128), 1)
    return jnp.sum(jnp.where(eye, jnp.broadcast_to(row, (128, 128)), 0.0), axis=1, keepdims=True)


def ids_and_places(ids_ref, chunk):
    base = pl.multiple_of(chunk * 128, 128)
    own = ids_ref[:, pl.ds(pl.multiple_of(base + SPAN, 128), 128)].astype(F32)
    col = column(own)
    total = jnp.zeros((128, 128), F32)
    for k in range(SPAN // 128 + 1):
        part = ids_ref[:, pl.ds(pl.multiple_of(base + k * 128, 128), 128)].astype(F32)
        total = total + jnp.where(jnp.broadcast_to(part, (128, 128)) < col, 1.0, 0.0)
    before = jnp.sum(total, axis=1, keepdims=True)
    place = (SPAN + iota((128, 1), 0)).astype(F32) - before
    return col, place


def turn(high, low, tab_ref):
    rows = high.shape[0]
    parts = []
    for which, value in enumerate((high, low)):
        hot = jnp.where(iota((rows, 32), 1).astype(F32) == value, 1.0, 0.0).astype(BF)
        got = mm(hot, tab_ref[which])
        parts.append(got[:, :256] + got[:, 256:512] + got[:, 512:])
    (ch, sh), (cl, sl) = [(p[:, :128], p[:, 128:]) for p in parts]
    first = lax.rem(iota((1, 128), 1), 64) < 32
    sine = sh * cl + ch * sl
    return ch * cl - sh * sl, jnp.where(first, -sine, sine)


def rotated(part, cosine, sine):
    first = lax.rem(iota((1, 128), 1), 64) < 32
    other = jnp.where(first, pltpu.roll(part, 96, 1), pltpu.roll(part, 32, 1))
    return part * cosine + other * sine


def split_place(place):
    high = jnp.floor(place * (1.0 / 32.0))
    return high, place - 32.0 * high


def slots_kernel(tok_ref, owner_row, ids_ref, slots_ref, info_ref, wide, stage, place_all):
    pages = BLK // PAGE
    owner = owner_row[...].astype(F32)
    eye = iota((pages, pages), 0) == iota((pages, pages), 1)
    owner_col = jnp.sum(jnp.where(eye, jnp.broadcast_to(owner, (pages, pages)), 0.0), axis=1, keepdims=True)
    same = owner_col == owner
    earlier = iota((pages, pages), 0) < iota((pages, pages), 1)
    rank = jnp.sum(jnp.where(same & earlier, 1.0, 0.0), axis=0, keepdims=True)
    target = owner * CAP + rank
    hot = jnp.where(iota((N_TOK * CAP, pages), 0).astype(F32) == target, 1.0, 0.0).astype(BF)
    for k in range(D // 128):
        wide[k] = tok_ref[:, k * 128 : k * 128 + 128].astype(F32)
    for t in range(PAGE):
        part = jnp.concatenate([wide[k, pl.ds(t, pages, stride=PAGE), :] for k in range(D // 128)], axis=1)
        placed = mm(hot, part.astype(BF))
        for k in range(D // 128):
            stage[k % 4, pl.ds(k // 4 * 4 + t, N_TOK * CAP, stride=8), :] = placed[:, k * 128 : k * 128 + 128]
    for k in range(4):
        slots_ref[:, k * 128 : k * 128 + 128] = stage[k].astype(BF)
    for k in range(BLK // 128):
        _, place = ids_and_places(ids_ref, BLK * REACH // 128 + k)
        place_all[pl.ds(k * 128, 128), :] = jnp.broadcast_to(place, (128, 128))
    lane = iota((pages, 128), 1)
    info = jnp.zeros((N_TOK, 128), F32)
    for r in range(CAP):
        packed = jnp.zeros((pages, 128), F32)
        for t in range(PAGE):
            high, low = split_place(place_all[pl.ds(t, pages, stride=PAGE), :])
            packed = jnp.where(lane == r * 8 + t * 2, high, packed)
            packed = jnp.where(lane == r * 8 + t * 2 + 1, low, packed)
        pick = jnp.where((iota((N_TOK, pages), 0) * CAP + r).astype(F32) == target, 1.0, 0.0)
        info = info + mm(pick.astype(BF), packed.astype(BF))
    info_ref[...] = info[:, None, :]


def build_slots(tokens, owner_row, ids_row):
    return pl.pallas_call(
        slots_kernel,
        out_shape=(
            jax.ShapeDtypeStruct((N_TOK * CAP * 8, 512), BF),
            jax.ShapeDtypeStruct((N_TOK, 1, 128), F32),
        ),
        in_specs=[VMEM] * 3,
        out_specs=[VMEM] * 2,
        scratch_shapes=[
            pltpu.VMEM((D // 128, BLK, 128), F32),
            pltpu.VMEM((4, N_TOK * CAP * 8, 128), F32),
            pltpu.VMEM((BLK, 128), F32),
        ],
    )(tokens, owner_row, ids_row)


PAIRS = 4


def main_kernel(bounds, window_ref, wqkv_hbm, wo_hbm, ids_ref, gain_ref, tab_ref, slots_hbm, info_ref,
                out_ref, cache_ref,
                tok, wqkv, wo, keys, values, marks, heads, scores, mixed, slots, stage, sems):
    own = pl.ds(REACH * BLK, BLK)
    before, after = pl.ds(0, REACH * BLK), pl.ds((REACH + 1) * BLK, REACH * BLK)
    copies = [
        pltpu.make_async_copy(window_ref.at[own], tok.at[own], sems.at[0]),
        pltpu.make_async_copy(wqkv_hbm.at[:, :D], wqkv.at[:, :D], sems.at[1]),
        pltpu.make_async_copy(wqkv_hbm.at[:, D:], wqkv.at[:, D:], sems.at[4]),
        pltpu.make_async_copy(window_ref.at[before], tok.at[before], sems.at[5]),
        pltpu.make_async_copy(window_ref.at[after], tok.at[after], sems.at[6]),
        pltpu.make_async_copy(slots_hbm, slots, sems.at[2]),
        pltpu.make_async_copy(wo_hbm, wo, sems.at[3]),
    ]
    for copy in copies:
        copy.start()
    gain = gain_ref[...]
    first_row = bounds[6]
    copies[0].wait()
    copies[1].wait()
    for t in range(3):
        here = pl.ds(REACH * BLK + t * 128, 128)
        normed = layer_norm(tok[here, :].astype(F32), gain).astype(BF)
        _, place = ids_and_places(ids_ref, REACH * 3 + t)
        cosine, sine = turn(*split_place(place), tab_ref)
        part = mm(normed, wqkv[:, :D])
        for pair in range(H // 2):
            turned = rotated(part[:, pair * 128 : pair * 128 + 128], cosine, sine)
            turned = turned.T.astype(BF).astype(F32) * 0.125
            upper = iota((128, 128), 0) < 64
            heads[t, pair, :, :128] = jnp.where(upper, turned, 0.0).astype(BF)
            heads[t, pair, :, 128:] = jnp.where(upper, 0.0, turned).astype(BF)
    for k in range(2, 5):
        copies[k].wait()
    low = bounds[0]
    count = (bounds[5] + 2 - low) // 2

    def project(i, _):
        chunk = low + i * 2
        start = pl.multiple_of(chunk * 128, 128)
        here = pl.ds(start, 256)
        local = start + iota((256, 1), 0)
        real = (local < WIN) & (local + first_row >= REACH * BLK) & (local + first_row < N_TOK * 4 * BLK + REACH * BLK)
        normed = jnp.where(real, layer_norm(tok[here, :].astype(F32), gain), 0.0).astype(BF)
        pieces = [ids_and_places(ids_ref, chunk + k) for k in range(2)]
        place = jnp.concatenate([p[1] for p in pieces], axis=0)
        for k in range(2):
            marks[pl.ds(pl.multiple_of(start + k * 128, 128), 128), :] = jnp.broadcast_to(pieces[k][0], (128, 128))
        cosine, sine = turn(*split_place(place), tab_ref)
        for part in range(2):
            got = mm(normed, wqkv[:, D + part * 512 : D + part * 512 + 512])
            for k in range(4):
                lanes = pl.ds(part * 512 + k * 128, 128)
                keys[here, lanes] = rotated(got[:, k * 128 : k * 128 + 128], cosine, sine).astype(BF)
        for part in range(2):
            got = mm(normed, wqkv[:, 2 * D + part * 512 : 2 * D + part * 512 + 512])
            for k in range(4):
                lane = part * 512 + k * 128
                values[pl.ds(lane, 128), here] = got[:, k * 128 : k * 128 + 128].T.astype(BF)
        return 0

    lax.fori_loop(0, count, project, 0)
    fold = lambda op, value: op(value.reshape(32, 8, 128), axis=0)
    for t in range(3):
        id_row = ids_ref[:, pl.ds(SPAN + REACH * BLK + t * 128, 128)].astype(F32)
        begin = bounds[t]
        steps = (bounds[3 + t] - begin + 1) // 2

        def pairs(group, _):
            lane0 = [pl.multiple_of((group * PAIRS + j) * 128, 128) for j in range(PAIRS)]

            def score(i, peaks):
                start = pl.multiple_of((begin + i * 2) * 128, 128)
                allowed = marks[pl.ds(start, 256), :] == id_row
                new = []
                for j in range(PAIRS):
                    got = mm(keys[pl.ds(start, 256), pl.ds(lane0[j], 128)], heads[t, group * PAIRS + j])
                    for side in range(2):
                        half = jnp.where(allowed, got[:, side * 128 : side * 128 + 128], NEG_FILL)
                        scores[j, i, side] = half
                        new.append(jnp.maximum(peaks[2 * j + side], fold(jnp.max, half)))
                return tuple(new)

            peaks = lax.fori_loop(0, steps, score, (jnp.full((8, 128), NEG_FILL, F32),) * (2 * PAIRS))
            peaks = [jnp.max(p, axis=0, keepdims=True) for p in peaks]

            def mix(i, carry):
                start = pl.multiple_of((begin + i * 2) * 128, 128)
                totals, accs = [], []
                for j in range(PAIRS):
                    both = []
                    for side in range(2):
                        weight = jnp.exp(scores[j, i, side] - peaks[2 * j + side])
                        totals.append(carry[2 * j + side] + fold(jnp.sum, weight))
                        both.append(weight.astype(BF))
                    accs.append(carry[2 * PAIRS + j] + mm(
                        values[pl.ds(lane0[j], 128), pl.ds(start, 256)], jnp.concatenate(both, axis=1)))
                return tuple(totals + accs)

            done = lax.fori_loop(
                0, steps, mix, (jnp.zeros((8, 128), F32),) * (2 * PAIRS) + (jnp.zeros((128, 256), F32),) * PAIRS)
            for j in range(PAIRS):
                total = [jnp.sum(done[2 * j + side], axis=0, keepdims=True) for side in range(2)]
                acc = done[2 * PAIRS + j]
                upper = iota((128, 128), 0) < 64
                picked = jnp.where(upper, acc[:, :128] / total[0], acc[:, 128:] / total[1])
                mixed[pl.ds(t * 128, 128), pl.ds(lane0[j], 128)] = picked.T.astype(BF)
            return 0

        lax.fori_loop(0, H // 2 // PAIRS, pairs, 0)
    copies[6].wait()
    out_ref[...] = mm(mixed[...], wo[...]).astype(BF)
    copies[5].wait()
    for k in range(4):
        stage[k] = slots[:, k * 128 : k * 128 + 128].astype(F32)
    count_slots = N_TOK * CAP
    info = info_ref[:, 0, :].astype(BF)
    lane = iota((count_slots, 128), 1)
    spread = []
    for r in range(CAP):
        pick = iota((count_slots, N_TOK), 0) == iota((count_slots, N_TOK), 1) * CAP + r
        spread.append(mm(jnp.where(pick, 1.0, 0.0).astype(BF), info))

    for t in range(PAGE):
        sides = [stage[k % 4, pl.ds(k // 4 * 4 + t, count_slots, stride=8), :] for k in range(8)]
        normed = layer_norm(jnp.concatenate(sides, axis=1), gain).astype(BF)
        parts = []
        for side in range(2):
            found = jnp.zeros((count_slots, 128), F32)
            for r in range(CAP):
                found = found + jnp.where(lane == r * 8 + t * 2 + side, spread[r], 0.0)
            parts.append(jnp.sum(found, axis=1, keepdims=True))
        cosine, sine = turn(*parts, tab_ref)
        got = mm(normed, wqkv[:, D : 2 * D])
        for k in range(8):
            cache_ref[:, pl.ds(t * 2048 + k * 128, 128)] = rotated(
                got[:, k * 128 : k * 128 + 128], cosine, sine).astype(BF)
        cache_ref[:, pl.ds(t * 2048 + D, D)] = mm(normed, wqkv[:, 2 * D :]).astype(BF)


def main_call(bounds, window, wqkv, wo, ids_row, gain, tables, slots, info):
    return pl.pallas_call(
        main_kernel,
        out_shape=(
            jax.ShapeDtypeStruct((BLK, D), BF),
            jax.ShapeDtypeStruct((N_TOK * CAP, 2 * PAGE * D), BF),
        ),
        in_specs=[SMEM, ANY, ANY, ANY, VMEM, VMEM, VMEM, ANY, VMEM],
        out_specs=[VMEM] * 2,
        scratch_shapes=[
            pltpu.VMEM((WIN + EXTRA, D), BF),
            pltpu.VMEM((D, 3 * D), BF),
            pltpu.VMEM((D, D), BF),
            pltpu.VMEM((WIN + EXTRA, D), BF),
            pltpu.VMEM((D, WIN + EXTRA), BF),
            pltpu.VMEM((WIN + EXTRA, 128), F32),
            pltpu.VMEM((3, H // 2, 128, 256), BF),
            pltpu.VMEM((PAIRS, 11, 2, 256, 128), F32),
            pltpu.VMEM((BLK, D), BF),
            pltpu.VMEM((N_TOK * CAP * 8, 512), BF),
            pltpu.VMEM((4, N_TOK * CAP * 8, 128), F32),
            pltpu.SemaphoreType.DMA((7,)),
        ],
        compiler_params=pltpu.CompilerParams(vmem_limit_bytes=60 * 1024 * 1024),
    )(bounds, window, wqkv, wo, ids_row, gain, tables, slots, info)


def remote(src, dst, ssem, rsem, tok, grp):
    return pltpu.make_async_remote_copy(src_ref=src, dst_ref=dst, send_sem=ssem, recv_sem=rsem,
                                        device_id=(tok, grp), device_id_type=MESH)

CUT = (1, 12, 20, 28, 36, 64)


def comm_kernel(tok_ref, win_ref, wout_ref, slots_ref, place_ref,
                wqkv_ref, wo_ref, window_ref, slots_out, place_out, outer_ref,
                xs, xr, zs, zr, ys, yr, hs, hr, bs, br, ts, tr, us, ur, ns, nr, os, fs, fr, ps, pr, loc):
    do = {"weights": True, "tokens": True, "pages": True}
    a = lax.axis_index("tok"); x = lax.axis_index("grp")
    c = lax.rem(a, 2); z = lax.rem(a // 2, NZ); y = a // (2 * NZ)
    tok_of = lambda yy, zz, cc: (yy * NZ + zz) * 2 + cc
    ring = lambda v, d, n: lax.rem(v + d + n, n)
    sib = a + 1 - 2 * c
    n_tok = NY * NZ * 2
    barrier = pltpu.get_barrier_semaphore()

    def greet(j, _):
        pl.semaphore_signal(barrier, inc=1, device_id=(lax.rem(a + j, n_tok), x), device_id_type=MESH)
        return 0
    lax.fori_loop(1, n_tok, greet, 0)
    for d in range(1, 4):
        pl.semaphore_signal(barrier, inc=1, device_id=(a, lax.rem(x + d, 4)), device_id_type=MESH)
    pl.semaphore_wait(barrier, n_tok - 1 + 3)

    full = (wqkv_ref, wo_ref)
    shard = (win_ref, wout_ref)
    width = (768, 256)
    W = (0, 1)
    rows_of = lambda aa: pl.ds(pl.multiple_of(aa * 16, 16), 16)
    half_rows = lambda aa, h: pl.ds(pl.multiple_of(aa * 16 + 8 * h, 8), 8)
    block = lambda w, aa: full[w].at[rows_of(aa)]
    half = lambda w, aa, h: full[w].at[half_rows(aa, h)]
    piece = lambda w, aa, xx: full[w].at[rows_of(aa), pl.ds(pl.multiple_of(xx * width[w], 128), width[w])]
    xp, xm, xo = ring(x, 1, 4), ring(x, -1, 4), ring(x, 2, 4)
    widx = lambda xx, at: 3 + xx - at
    taken = lambda ref, sem: remote(ref, ref, sem, sem, a, xp).wait_recv()
    left = lambda ref, sem: remote(ref, ref, sem, sem, a, xp).wait_send()

    def z_send(w, zz, dirn, src=None):
        here = piece(w, tok_of(y, zz, c), x)
        remote(here if src is None else src, here, zs.at[w, dirn, zz], zr.at[w, zz],
               tok_of(y, ring(z, 1 - 2 * dirn, NZ), c), x).start()
    def x_send(w, zz, src=None):
        here = piece(w, tok_of(y, zz, c), x)
        for d in range(1, 4):
            remote(here if src is None else src, here, xs.at[w, d - 1, zz], xr.at[w, d - 1, zz], a, ring(x, d, 4)).start()
    def sib_send(w, yy, zz):
        blk = block(w, tok_of(yy, zz, c))
        remote(blk, blk, bs.at[w, yy, zz], br.at[w, yy, zz], sib, x).start()
    def join(w, zz):
        for d in range(1, 4):
            taken(piece(w, tok_of(y, zz, c), ring(x, -d, 4)), xr.at[w, d - 1, zz])
        blk = block(w, tok_of(y, zz, c))
        remote(blk, blk, ys.at[w, 0, zz], yr.at[w, 0, zz], tok_of(ring(y, 1, NY), z, c), x).start()
        remote(blk, blk, ys.at[w, 1, zz], yr.at[w, 1, zz], tok_of(ring(y, -1, NY), z, c), x).start()
        sib_send(w, y, zz)
    def y_relay(w, zz):
        ym, yp = ring(y, -1, NY), ring(y, 1, NY)
        taken(block(w, tok_of(ym, zz, c)), yr.at[w, 0, zz])
        h = half(w, tok_of(ym, zz, c), 0)
        remote(h, h, hs.at[w, 0, zz], hr.at[w, 0, zz], tok_of(yp, z, c), x).start()
        sib_send(w, ym, zz)
        taken(block(w, tok_of(yp, zz, c)), yr.at[w, 1, zz])
        h = half(w, tok_of(yp, zz, c), 1)
        remote(h, h, hs.at[w, 1, zz], hr.at[w, 1, zz], tok_of(ym, z, c), x).start()
        sib_send(w, yp, zz)
    def y_last(w, zz):
        yo = ring(y, 2, NY)
        taken(half(w, tok_of(yo, zz, c), 0), hr.at[w, 0, zz])
        taken(half(w, tok_of(yo, zz, c), 1), hr.at[w, 1, zz])
        sib_send(w, yo, zz)
    def z_step(k):
        zp, zm = ring(z, -k, NZ), lax.rem(z + k, NZ)
        for w in W:
            taken(piece(w, tok_of(y, zp, c), x), zr.at[w, zp])
            if k < 4: z_send(w, zp, 0)
        if k < 4:
            for w in W:
                taken(piece(w, tok_of(y, zm, c), x), zr.at[w, zm])
                if k < 3: z_send(w, zm, 1)
        for w in W:
            x_send(w, zp)
            if k < 4: x_send(w, zm)
    def joins(k):
        for w in W: join(w, ring(z, -k, NZ))
        if 0 < k < 4:
            for w in W: join(w, lax.rem(z + k, NZ))

    sgn = 1 - 2 * c
    u = jnp.where(c == 0, x, 3 - x)
    at_u = lambda v: jnp.where(c == 0, v, 3 - v)
    far = a - sgn
    linked = (far >= 0) & (far < n_tok)
    fidx = lambda uu, at: (at_u(uu) - at_u(at)) - 1 + 8 * c
    hb = BLK // 2
    top, bot = pl.ds(0, hb), pl.ds(hb, hb)
    def cross(xx, k):
        @pl.when((xx - x) * sgn > 0)
        def _():
            remote(window_ref.at[widx(xx, x)], window_ref.at[xx - x - 1 + 8 * c], ns.at[k], nr.at[k], sib, x).start()
    def outer_on():
        @pl.when(linked & (u >= 1))
        def _():
            taken(outer_ref, os.at[1])
            remote(outer_ref, window_ref.at[fidx(u, u - 1)], fs.at[0], fr.at[0], a, at_u(u - 1)).start()
        @pl.when(linked & (u == 3))
        def _():
            remote(outer_ref, window_ref.at[fidx(3, 0)], fs.at[1], fr.at[1], a, at_u(0)).start()
    def outer_relay():
        @pl.when(linked & (u <= 2))
        def _():
            taken(window_ref.at[fidx(u + 1, u)], fr.at[0])
        @pl.when(linked & (u >= 1) & (u <= 2))
        def _():
            remote(window_ref.at[fidx(u + 1, u)], window_ref.at[fidx(u + 1, u - 1)], fs.at[2], fr.at[2], a, at_u(u - 1)).start()
    def ring_relay():
        taken(window_ref.at[widx(xm, x)], tr.at[0])
        remote(window_ref.at[widx(xm, x), top], window_ref.at[widx(xm, xp), top], us.at[0], ur.at[0], a, xp).start()
        taken(window_ref.at[widx(xp, x)], tr.at[1])
        remote(window_ref.at[widx(xp, x), bot], window_ref.at[widx(xp, xm), bot], us.at[1], ur.at[1], a, xm).start()
        cross(xm, 0); cross(xp, 1)

    mine = pl.ds(a * 3, 3)
    def send_pages(lo, hi):
        if not do["pages"]: return
        def one(j, _):
            peer = lax.rem(a + lax.rem(j * 27, n_tok), n_tok)
            remote(slots_ref.at[pl.ds(peer * 3, 3)], slots_out.at[mine], ps.at[0], pr.at[0], peer, x).start()
            remote(place_ref.at[peer], place_out.at[a], ps.at[1], pr.at[1], peer, x).start()
            return 0
        lax.fori_loop(lo, hi, one, 0)

    if do["weights"]:
        for w in W:
            pltpu.make_async_copy(shard[w], piece(w, a, x), loc.at[w]).start()
            z_send(w, z, 0, shard[w]); z_send(w, z, 1, shard[w])
            x_send(w, z, shard[w])
    if do["tokens"]:
        pltpu.make_async_copy(tok_ref, window_ref.at[3], loc.at[2]).start()
        @pl.when(linked & (u <= 2))
        def _(): remote(tok_ref, outer_ref, os.at[0], os.at[1], far, x).start()
        remote(tok_ref, window_ref.at[widx(x, xp)], ts.at[0], tr.at[0], a, xp).start()
        remote(tok_ref, window_ref.at[widx(x, xm)], ts.at[1], tr.at[1], a, xm).start()
    if do["pages"]:
        pltpu.make_async_copy(slots_ref.at[mine], slots_out.at[mine], loc.at[3]).start()
        pltpu.make_async_copy(place_ref.at[a], place_out.at[a], loc.at[4]).start()
    send_pages(CUT[0], CUT[1])
    if do["weights"]:
        for w in W: pltpu.make_async_copy(shard[w], piece(w, a, x), loc.at[w]).wait()
        z_step(1); joins(0)
    send_pages(CUT[1], CUT[2])
    if do["weights"]:
        z_step(2); joins(1)
    send_pages(CUT[2], CUT[3])
    if do["weights"]: z_step(3)
    if do["tokens"]: outer_on()
    send_pages(CUT[3], CUT[4])
    if do["weights"]:
        joins(2); z_step(4)
    send_pages(CUT[4], CUT[5])
    if do["tokens"]: ring_relay()
    if do["weights"]:
        joins(3)
    order = lambda i: lax.rem(z + jnp.where(lax.rem(i, 2) == 1, NZ - (i + 1) // 2, i // 2), NZ)
    def relays(lo, hi):
        def relay(i, _):
            for w in W: y_relay(w, order(i))
            return 0
        lax.fori_loop(lo, hi, relay, 0)
    if do["weights"]:
        relays(0, 2)
        joins(4)
    if do["tokens"]: outer_relay()
    if do["weights"]: relays(2, 5)
    if do["tokens"]:
        taken(window_ref.at[widx(xo, x), top], ur.at[0])
        taken(window_ref.at[widx(xo, x), bot], ur.at[1])
        cross(xo, 2)
    if do["weights"]:
        relays(5, NZ)
        def last(i, _):
            for w in W: y_last(w, order(i))
            return 0
        lax.fori_loop(0, NZ, last, 0)
        def sibs(i, _):
            yy, zz = i // NZ, lax.rem(i, NZ)
            for w in W:
                taken(block(w, tok_of(yy, zz, 1 - c)), br.at[w, yy, zz])
                left(block(w, tok_of(yy, zz, c)), bs.at[w, yy, zz])
            return 0
        lax.fori_loop(0, NY * NZ, sibs, 0)
        def drain(zz, _):
            for w in W:
                for d in range(2):
                    left(block(w, a), ys.at[w, d, zz])
                    left(half(w, a, 0), hs.at[w, d, zz])
                for d in range(3):
                    left(piece(w, a, x), xs.at[w, d, zz])
            return 0
        lax.fori_loop(0, NZ, drain, 0)
        for k in range(4):
            for w in W:
                left(piece(w, a, x), zs.at[w, 0, ring(z, -k, NZ)])
                if k < 3: left(piece(w, a, x), zs.at[w, 1, lax.rem(z + k, NZ)])
    if do["tokens"]:
        blk = window_ref.at[3]
        hv = window_ref.at[3, top]
        for d in range(2):
            left(blk, ts.at[d]); left(hv, us.at[d])
        pltpu.make_async_copy(tok_ref, window_ref.at[3], loc.at[2]).wait()
        for k, xx in enumerate((xm, xp, xo)):
            @pl.when((xx - x) * sgn > 0)
            def _(): left(blk, ns.at[k])
            @pl.when((xx - x) * sgn < 0)
            def _(): taken(window_ref.at[xx - x + 7 - 8 * c], nr.at[k])
        @pl.when(linked & (u <= 2))
        def _(): left(blk, os.at[0])
        @pl.when(linked & (u >= 1))
        def _(): left(blk, fs.at[0])
        @pl.when(linked & (u == 3))
        def _(): left(blk, fs.at[1])
        @pl.when(linked & (u >= 1) & (u <= 2))
        def _(): left(blk, fs.at[2])
        @pl.when(linked & (u == 0))
        def _(): taken(window_ref.at[fidx(3, 0)], fr.at[1])
        @pl.when(linked & (u <= 1))
        def _(): taken(window_ref.at[fidx(u + 2, u)], fr.at[2])
    if do["pages"]:
        pltpu.make_async_copy(slots_ref.at[mine], slots_out.at[mine], loc.at[3]).wait()
        pltpu.make_async_copy(place_ref.at[a], place_out.at[a], loc.at[4]).wait()
        rest = pl.ds(0, (n_tok - 1) * 3)
        prest = pl.ds(0, n_tok - 1)
        remote(slots_ref.at[rest], slots_out.at[rest], ps.at[0], pr.at[0], a, xp).wait()
        remote(place_ref.at[prest], place_out.at[prest], ps.at[1], pr.at[1], a, xp).wait()

def comm(tokens, w_in, w_out, slots, place):
    D_ = pltpu.SemaphoreType.DMA
    return pl.pallas_call(
        comm_kernel,
        out_shape=(jax.ShapeDtypeStruct((1024, 3072), BF), jax.ShapeDtypeStruct((1024, 1024), BF),
                   jax.ShapeDtypeStruct((7, tokens.shape[0], 1024), BF),
                   jax.ShapeDtypeStruct(slots.shape, BF), jax.ShapeDtypeStruct(place.shape, place.dtype),
                   jax.ShapeDtypeStruct(tokens.shape, BF)),
        in_specs=[ANY] * 5, out_specs=[ANY] * 6,
        scratch_shapes=[D_((2, 3, NZ)), D_((2, 3, NZ)), D_((2, 2, NZ)), D_((2, NZ)), D_((2, 2, NZ)), D_((2, 2, NZ)),
                        D_((2, 2, NZ)), D_((2, 2, NZ)), D_((2, NY, NZ)), D_((2, NY, NZ)), D_((2,)), D_((2,)), D_((2,)), D_((2,)),
                        D_((3,)), D_((3,)), D_((2,)), D_((3,)), D_((3,)), D_((2,)), D_((2,)), D_((5,))],
        compiler_params=pltpu.CompilerParams(collective_id=0, has_side_effects=True),
    )(tokens, w_in, w_out, slots, place)[:5]


def per_device(tokens, norm_gain, input_weight, output_weight, segment_ids, page_owner, tables):
    device = lax.axis_index("tok") * 4 + lax.axis_index("grp")
    first_row = device * BLK
    ahead = SPAN + REACH * BLK
    padded = jnp.concatenate([
        jnp.full((ahead,), -1, jnp.int32), segment_ids, jnp.full((REACH * BLK + EXTRA,), TOP, jnp.int32)])
    ids = lax.dynamic_slice_in_dim(padded, first_row, SPAN + WIN + EXTRA, 0)
    reach = ids[SPAN : SPAN + WIN]
    own = reach[REACH * BLK : (REACH + 1) * BLK].reshape(3, 128)
    begin = jnp.sum((reach[None, :] < own[:, :1]).astype(jnp.int32), axis=1) // 128
    end = (jnp.sum((reach[None, :] <= own[:, 127:]).astype(jnp.int32), axis=1) + 127) // 128
    bounds = jnp.concatenate([begin, end, first_row[None], first_row[None]])
    ids_row = ids[None, :]
    slots, info = build_slots(tokens, page_owner.reshape(1, -1), ids_row)
    wqkv, wo, window, slots, info = comm(tokens, input_weight, output_weight, slots.reshape(N_TOK * CAP, 8, 512), info)
    return main_call(bounds, window.reshape(WIN, D), wqkv, wo, ids_row, norm_gain[None, :], tables,
                     slots.reshape(N_TOK * CAP * 8, 512), info)


def solution(mesh):
    placed = (
        P(("tok", "grp"), None),
        P(),
        P("tok", "grp"),
        P("tok", "grp"),
        P(),
        P(("tok", "grp"), None),
        P(),
    )
    tables = rope_tables()
    step = jax.shard_map(
        per_device,
        mesh=mesh,
        in_specs=placed,
        out_specs=(P(("tok", "grp"), None), P(("tok", "grp"), None)),
        check_vma=False,
    )
    return lambda *args: step(*args, jnp.asarray(tables))
```

```python
import functools

import jax
import jax.numpy as jnp
import ml_dtypes
import numpy as np
from jax import lax
from jax.experimental import pallas as pl
from jax.experimental.pallas import tpu as pltpu
from jax.sharding import PartitionSpec as P

D = 1024
H = 16
SPAN = 1024
PAGE = 4
CAP = 3
BLK = 384
REACH = 3
WIN = (2 * REACH + 1) * BLK
EXTRA = 256
NEG_FILL = -1e30
ROPE_BASE = 160000.0
EPSILON = 1e-5
N_TOK = 64
NY, NZ = 4, 8
ROWS = 16
TOP = 1 << 30

MESH = pl.DeviceIdType.MESH
ANY = pl.BlockSpec(memory_space=pl.ANY)
VMEM = pl.BlockSpec(memory_space=pltpu.VMEM)
SMEM = pl.BlockSpec(memory_space=pltpu.SMEM)
BF, F32 = jnp.bfloat16, jnp.float32


def rope_tables():
    freq = 1.0 / ROPE_BASE ** (np.arange(32) * 2.0 / 64)
    lanes = np.tile(freq, 4)
    out = []
    for step in (32.0, 1.0):
        angle = step * np.arange(32)[:, None] * lanes[None, :]
        rest = np.concatenate([np.cos(angle), np.sin(angle)], axis=1)
        terms = []
        for _ in range(3):
            term = rest.astype(ml_dtypes.bfloat16)
            terms.append(term)
            rest = rest - term.astype(np.float64)
        out.append(np.concatenate(terms, axis=1))
    return np.stack(out)


def mm(left, right):
    return jnp.dot(left, right, preferred_element_type=F32)


def layer_norm(values, gain):
    center = jnp.mean(values, axis=-1, keepdims=True)
    moved = values - center
    spread = jnp.mean(jnp.square(moved), axis=-1, keepdims=True)
    return moved * lax.rsqrt(spread + EPSILON) * gain


def iota(shape, axis):
    return lax.broadcasted_iota(jnp.int32, shape, axis)


def column(row):
    eye = iota((128, 128), 0) == iota((128, 128), 1)
    return jnp.sum(jnp.where(eye, jnp.broadcast_to(row, (128, 128)), 0.0), axis=1, keepdims=True)


def ids_and_places(ids_ref, chunk):
    base = pl.multiple_of(chunk * 128, 128)
    own = ids_ref[:, pl.ds(pl.multiple_of(base + SPAN, 128), 128)].astype(F32)
    col = column(own)
    total = jnp.zeros((128, 128), F32)
    for k in range(SPAN // 128 + 1):
        part = ids_ref[:, pl.ds(pl.multiple_of(base + k * 128, 128), 128)].astype(F32)
        total = total + jnp.where(jnp.broadcast_to(part, (128, 128)) < col, 1.0, 0.0)
    before = jnp.sum(total, axis=1, keepdims=True)
    place = (SPAN + iota((128, 1), 0)).astype(F32) - before
    return col, place


def turn(high, low, tab_ref):
    rows = high.shape[0]
    parts = []
    for which, value in enumerate((high, low)):
        hot = jnp.where(iota((rows, 32), 1).astype(F32) == value, 1.0, 0.0).astype(BF)
        got = mm(hot, tab_ref[which])
        parts.append(got[:, :256] + got[:, 256:512] + got[:, 512:])
    (ch, sh), (cl, sl) = [(p[:, :128], p[:, 128:]) for p in parts]
    first = lax.rem(iota((1, 128), 1), 64) < 32
    sine = sh * cl + ch * sl
    return ch * cl - sh * sl, jnp.where(first, -sine, sine)


def rotated(part, cosine, sine):
    first = lax.rem(iota((1, 128), 1), 64) < 32
    other = jnp.where(first, pltpu.roll(part, 96, 1), pltpu.roll(part, 32, 1))
    return part * cosine + other * sine


def split_place(place):
    high = jnp.floor(place * (1.0 / 32.0))
    return high, place - 32.0 * high


def slots_kernel(tok_ref, owner_row, ids_ref, slots_ref, info_ref, wide, stage, place_all):
    pages = BLK // PAGE
    owner = owner_row[...].astype(F32)
    eye = iota((pages, pages), 0) == iota((pages, pages), 1)
    owner_col = jnp.sum(jnp.where(eye, jnp.broadcast_to(owner, (pages, pages)), 0.0), axis=1, keepdims=True)
    same = owner_col == owner
    earlier = iota((pages, pages), 0) < iota((pages, pages), 1)
    rank = jnp.sum(jnp.where(same & earlier, 1.0, 0.0), axis=0, keepdims=True)
    target = owner * CAP + rank
    hot = jnp.where(iota((N_TOK * CAP, pages), 0).astype(F32) == target, 1.0, 0.0).astype(BF)
    for k in range(D // 128):
        wide[k] = tok_ref[:, k * 128 : k * 128 + 128].astype(F32)
    for t in range(PAGE):
        part = jnp.concatenate([wide[k, pl.ds(t, pages, stride=PAGE), :] for k in range(D // 128)], axis=1)
        placed = mm(hot, part.astype(BF))
        for k in range(D // 128):
            stage[k % 4, pl.ds(k // 4 * 4 + t, N_TOK * CAP, stride=8), :] = placed[:, k * 128 : k * 128 + 128]
    for k in range(4):
        slots_ref[:, k * 128 : k * 128 + 128] = stage[k].astype(BF)
    for k in range(BLK // 128):
        _, place = ids_and_places(ids_ref, BLK * REACH // 128 + k)
        place_all[pl.ds(k * 128, 128), :] = jnp.broadcast_to(place, (128, 128))
    lane = iota((pages, 128), 1)
    info = jnp.zeros((N_TOK, 128), F32)
    for r in range(CAP):
        packed = jnp.zeros((pages, 128), F32)
        for t in range(PAGE):
            high, low = split_place(place_all[pl.ds(t, pages, stride=PAGE), :])
            packed = jnp.where(lane == r * 8 + t * 2, high, packed)
            packed = jnp.where(lane == r * 8 + t * 2 + 1, low, packed)
        pick = jnp.where((iota((N_TOK, pages), 0) * CAP + r).astype(F32) == target, 1.0, 0.0)
        info = info + mm(pick.astype(BF), packed.astype(BF))
    info_ref[...] = info[:, None, :]


def build_slots(tokens, owner_row, ids_row):
    return pl.pallas_call(
        slots_kernel,
        out_shape=(
            jax.ShapeDtypeStruct((N_TOK * CAP * 8, 512), BF),
            jax.ShapeDtypeStruct((N_TOK, 1, 128), F32),
        ),
        in_specs=[VMEM] * 3,
        out_specs=[VMEM] * 2,
        scratch_shapes=[
            pltpu.VMEM((D // 128, BLK, 128), F32),
            pltpu.VMEM((4, N_TOK * CAP * 8, 128), F32),
            pltpu.VMEM((BLK, 128), F32),
        ],
    )(tokens, owner_row, ids_row)


PAIRS = 8


def main_kernel(bounds, window_ref, wqkv_hbm, wo_hbm, ids_ref, gain_ref, tab_ref, slots_hbm, info_ref,
                out_ref, cache_ref,
                tok, wqkv, wo, keys, values, marks, heads, scores, mixed, slots, stage, sems):
    own = pl.ds(REACH * BLK, BLK)
    before, after = pl.ds(0, REACH * BLK), pl.ds((REACH + 1) * BLK, REACH * BLK)
    copies = [
        pltpu.make_async_copy(window_ref.at[own], tok.at[own], sems.at[0]),
        pltpu.make_async_copy(wqkv_hbm.at[:, :D], wqkv.at[:, :D], sems.at[1]),
        pltpu.make_async_copy(wqkv_hbm.at[:, D:], wqkv.at[:, D:], sems.at[4]),
        pltpu.make_async_copy(window_ref.at[before], tok.at[before], sems.at[5]),
        pltpu.make_async_copy(window_ref.at[after], tok.at[after], sems.at[6]),
        pltpu.make_async_copy(slots_hbm, slots, sems.at[2]),
        pltpu.make_async_copy(wo_hbm, wo, sems.at[3]),
    ]
    for copy in copies:
        copy.start()
    gain = gain_ref[...]
    first_row = bounds[6]
    copies[0].wait()
    copies[1].wait()
    for t in range(3):
        here = pl.ds(REACH * BLK + t * 128, 128)
        normed = layer_norm(tok[here, :].astype(F32), gain).astype(BF)
        _, place = ids_and_places(ids_ref, REACH * 3 + t)
        cosine, sine = turn(*split_place(place), tab_ref)
        part = mm(normed, wqkv[:, :D])
        for pair in range(H // 2):
            turned = rotated(part[:, pair * 128 : pair * 128 + 128], cosine, sine)
            turned = turned.T.astype(BF).astype(F32) * 0.125
            upper = iota((128, 128), 0) < 64
            heads[t, pair, :, :128] = jnp.where(upper, turned, 0.0).astype(BF)
            heads[t, pair, :, 128:] = jnp.where(upper, 0.0, turned).astype(BF)
    for k in range(2, 5):
        copies[k].wait()
    low = bounds[0]
    count = (bounds[5] + 2 - low) // 2

    def project(i, _):
        chunk = low + i * 2
        start = pl.multiple_of(chunk * 128, 128)
        here = pl.ds(start, 256)
        local = start + iota((256, 1), 0)
        real = (local < WIN) & (local + first_row >= REACH * BLK) & (local + first_row < N_TOK * 4 * BLK + REACH * BLK)
        normed = jnp.where(real, layer_norm(tok[here, :].astype(F32), gain), 0.0).astype(BF)
        pieces = [ids_and_places(ids_ref, chunk + k) for k in range(2)]
        place = jnp.concatenate([p[1] for p in pieces], axis=0)
        for k in range(2):
            marks[pl.ds(pl.multiple_of(start + k * 128, 128), 128), :] = jnp.broadcast_to(pieces[k][0], (128, 128))
        cosine, sine = turn(*split_place(place), tab_ref)
        for part in range(2):
            got = mm(normed, wqkv[:, D + part * 512 : D + part * 512 + 512])
            for k in range(4):
                lanes = pl.ds(part * 512 + k * 128, 128)
                keys[here, lanes] = rotated(got[:, k * 128 : k * 128 + 128], cosine, sine).astype(BF)
        for part in range(2):
            got = mm(normed, wqkv[:, 2 * D + part * 512 : 2 * D + part * 512 + 512])
            for k in range(4):
                lane = part * 512 + k * 128
                values[pl.ds(lane, 128), here] = got[:, k * 128 : k * 128 + 128].T.astype(BF)
        return 0

    lax.fori_loop(0, count, project, 0)
    fold = lambda op, value: op(value.reshape(32, 8, 128), axis=0)
    for t in range(3):
        id_row = ids_ref[:, pl.ds(SPAN + REACH * BLK + t * 128, 128)].astype(F32)
        begin = bounds[t]
        steps = (bounds[3 + t] - begin + 1) // 2

        def pairs(group, _):
            lane0 = [pl.multiple_of((group * PAIRS + j) * 128, 128) for j in range(PAIRS)]

            def score(i, peaks):
                start = pl.multiple_of((begin + i * 2) * 128, 128)
                allowed = marks[pl.ds(start, 256), :] == id_row
                new = []
                for j in range(PAIRS):
                    got = mm(keys[pl.ds(start, 256), pl.ds(lane0[j], 128)], heads[t, group * PAIRS + j])
                    for side in range(2):
                        half = jnp.where(allowed, got[:, side * 128 : side * 128 + 128], NEG_FILL)
                        scores[j, i, side] = half
                        new.append(jnp.maximum(peaks[2 * j + side], fold(jnp.max, half)))
                return tuple(new)

            peaks = lax.fori_loop(0, steps, score, (jnp.full((8, 128), NEG_FILL, F32),) * (2 * PAIRS))
            peaks = [jnp.max(p, axis=0, keepdims=True) for p in peaks]

            def mix(i, carry):
                start = pl.multiple_of((begin + i * 2) * 128, 128)
                totals, accs = [], []
                for j in range(PAIRS):
                    both = []
                    for side in range(2):
                        weight = jnp.exp(scores[j, i, side] - peaks[2 * j + side])
                        totals.append(carry[2 * j + side] + fold(jnp.sum, weight))
                        both.append(weight.astype(BF))
                    accs.append(carry[2 * PAIRS + j] + mm(
                        values[pl.ds(lane0[j], 128), pl.ds(start, 256)], jnp.concatenate(both, axis=1)))
                return tuple(totals + accs)

            done = lax.fori_loop(
                0, steps, mix, (jnp.zeros((8, 128), F32),) * (2 * PAIRS) + (jnp.zeros((128, 256), F32),) * PAIRS)
            for j in range(PAIRS):
                total = [jnp.sum(done[2 * j + side], axis=0, keepdims=True) for side in range(2)]
                acc = done[2 * PAIRS + j]
                upper = iota((128, 128), 0) < 64
                picked = jnp.where(upper, acc[:, :128] / total[0], acc[:, 128:] / total[1])
                mixed[pl.ds(t * 128, 128), pl.ds(lane0[j], 128)] = picked.T.astype(BF)
            return 0

        lax.fori_loop(0, H // 2 // PAIRS, pairs, 0)
    copies[6].wait()
    out_ref[...] = mm(mixed[...], wo[...]).astype(BF)
    copies[5].wait()
    for k in range(4):
        stage[k] = slots[:, k * 128 : k * 128 + 128].astype(F32)
    count_slots = N_TOK * CAP
    info = info_ref[:, 0, :].astype(BF)
    lane = iota((count_slots, 128), 1)
    spread = []
    for r in range(CAP):
        pick = iota((count_slots, N_TOK), 0) == iota((count_slots, N_TOK), 1) * CAP + r
        spread.append(mm(jnp.where(pick, 1.0, 0.0).astype(BF), info))

    for t in range(PAGE):
        sides = [stage[k % 4, pl.ds(k // 4 * 4 + t, count_slots, stride=8), :] for k in range(8)]
        normed = layer_norm(jnp.concatenate(sides, axis=1), gain).astype(BF)
        parts = []
        for side in range(2):
            found = jnp.zeros((count_slots, 128), F32)
            for r in range(CAP):
                found = found + jnp.where(lane == r * 8 + t * 2 + side, spread[r], 0.0)
            parts.append(jnp.sum(found, axis=1, keepdims=True))
        cosine, sine = turn(*parts, tab_ref)
        got = mm(normed, wqkv[:, D : 2 * D])
        for k in range(8):
            cache_ref[:, pl.ds(t * 2048 + k * 128, 128)] = rotated(
                got[:, k * 128 : k * 128 + 128], cosine, sine).astype(BF)
        cache_ref[:, pl.ds(t * 2048 + D, D)] = mm(normed, wqkv[:, 2 * D :]).astype(BF)


def main_call(bounds, window, wqkv, wo, ids_row, gain, tables, slots, info):
    return pl.pallas_call(
        main_kernel,
        out_shape=(
            jax.ShapeDtypeStruct((BLK, D), BF),
            jax.ShapeDtypeStruct((N_TOK * CAP, 2 * PAGE * D), BF),
        ),
        in_specs=[SMEM, ANY, ANY, ANY, VMEM, VMEM, VMEM, ANY, VMEM],
        out_specs=[VMEM] * 2,
        scratch_shapes=[
            pltpu.VMEM((WIN + EXTRA, D), BF),
            pltpu.VMEM((D, 3 * D), BF),
            pltpu.VMEM((D, D), BF),
            pltpu.VMEM((WIN + EXTRA, D), BF),
            pltpu.VMEM((D, WIN + EXTRA), BF),
            pltpu.VMEM((WIN + EXTRA, 128), F32),
            pltpu.VMEM((3, H // 2, 128, 256), BF),
            pltpu.VMEM((PAIRS, 9, 2, 256, 128), F32),
            pltpu.VMEM((BLK, D), BF),
            pltpu.VMEM((N_TOK * CAP * 8, 512), BF),
            pltpu.VMEM((4, N_TOK * CAP * 8, 128), F32),
            pltpu.SemaphoreType.DMA((7,)),
        ],
        compiler_params=pltpu.CompilerParams(vmem_limit_bytes=67043328),
    )(bounds, window, wqkv, wo, ids_row, gain, tables, slots, info)


def remote(src, dst, ssem, rsem, tok, grp):
    return pltpu.make_async_remote_copy(src_ref=src, dst_ref=dst, send_sem=ssem, recv_sem=rsem,
                                        device_id=(tok, grp), device_id_type=MESH)

CUT = (1, 12, 20, 28, 36, 64)


def comm_kernel(tok_ref, win_ref, wout_ref, slots_ref, place_ref,
                wqkv_ref, wo_ref, window_ref, slots_out, place_out, outer_ref,
                xs, xr, zs, zr, ys, yr, hs, hr, bs, br, ts, tr, us, ur, ns, nr, os, fs, fr, ps, pr, loc):
    do = {"weights": True, "tokens": True, "pages": True}
    a = lax.axis_index("tok"); x = lax.axis_index("grp")
    c = lax.rem(a, 2); z = lax.rem(a // 2, NZ); y = a // (2 * NZ)
    tok_of = lambda yy, zz, cc: (yy * NZ + zz) * 2 + cc
    ring = lambda v, d, n: lax.rem(v + d + n, n)
    sib = a + 1 - 2 * c
    n_tok = NY * NZ * 2
    barrier = pltpu.get_barrier_semaphore()

    def greet(j, _):
        pl.semaphore_signal(barrier, inc=1, device_id=(lax.rem(a + j, n_tok), x), device_id_type=MESH)
        return 0
    lax.fori_loop(1, n_tok, greet, 0)
    for d in range(1, 4):
        pl.semaphore_signal(barrier, inc=1, device_id=(a, lax.rem(x + d, 4)), device_id_type=MESH)
    pl.semaphore_wait(barrier, n_tok - 1 + 3)

    full = (wqkv_ref, wo_ref)
    shard = (win_ref, wout_ref)
    width = (768, 256)
    W = (0, 1)
    rows_of = lambda aa: pl.ds(pl.multiple_of(aa * 16, 16), 16)
    half_rows = lambda aa, h: pl.ds(pl.multiple_of(aa * 16 + 8 * h, 8), 8)
    block = lambda w, aa: full[w].at[rows_of(aa)]
    half = lambda w, aa, h: full[w].at[half_rows(aa, h)]
    piece = lambda w, aa, xx: full[w].at[rows_of(aa), pl.ds(pl.multiple_of(xx * width[w], 128), width[w])]
    xp, xm, xo = ring(x, 1, 4), ring(x, -1, 4), ring(x, 2, 4)
    widx = lambda xx, at: 3 + xx - at
    taken = lambda ref, sem: remote(ref, ref, sem, sem, a, xp).wait_recv()
    left = lambda ref, sem: remote(ref, ref, sem, sem, a, xp).wait_send()

    def z_send(w, zz, dirn, src=None):
        here = piece(w, tok_of(y, zz, c), x)
        remote(here if src is None else src, here, zs.at[w, dirn, zz], zr.at[w, zz],
               tok_of(y, ring(z, 1 - 2 * dirn, NZ), c), x).start()
    def x_send(w, zz, src=None):
        here = piece(w, tok_of(y, zz, c), x)
        for d in range(1, 4):
            remote(here if src is None else src, here, xs.at[w, d - 1, zz], xr.at[w, d - 1, zz], a, ring(x, d, 4)).start()
    def sib_send(w, yy, zz):
        blk = block(w, tok_of(yy, zz, c))
        remote(blk, blk, bs.at[w, yy, zz], br.at[w, yy, zz], sib, x).start()
    def join(w, zz):
        for d in range(1, 4):
            taken(piece(w, tok_of(y, zz, c), ring(x, -d, 4)), xr.at[w, d - 1, zz])
        blk = block(w, tok_of(y, zz, c))
        remote(blk, blk, ys.at[w, 0, zz], yr.at[w, 0, zz], tok_of(ring(y, 1, NY), z, c), x).start()
        remote(blk, blk, ys.at[w, 1, zz], yr.at[w, 1, zz], tok_of(ring(y, -1, NY), z, c), x).start()
        sib_send(w, y, zz)
    def y_relay(w, zz):
        ym, yp = ring(y, -1, NY), ring(y, 1, NY)
        taken(block(w, tok_of(ym, zz, c)), yr.at[w, 0, zz])
        h = half(w, tok_of(ym, zz, c), 0)
        remote(h, h, hs.at[w, 0, zz], hr.at[w, 0, zz], tok_of(yp, z, c), x).start()
        sib_send(w, ym, zz)
        taken(block(w, tok_of(yp, zz, c)), yr.at[w, 1, zz])
        h = half(w, tok_of(yp, zz, c), 1)
        remote(h, h, hs.at[w, 1, zz], hr.at[w, 1, zz], tok_of(ym, z, c), x).start()
        sib_send(w, yp, zz)
    def y_last(w, zz):
        yo = ring(y, 2, NY)
        taken(half(w, tok_of(yo, zz, c), 0), hr.at[w, 0, zz])
        taken(half(w, tok_of(yo, zz, c), 1), hr.at[w, 1, zz])
        sib_send(w, yo, zz)
    def z_step(k):
        zp, zm = ring(z, -k, NZ), lax.rem(z + k, NZ)
        for w in W:
            taken(piece(w, tok_of(y, zp, c), x), zr.at[w, zp])
            if k < 4: z_send(w, zp, 0)
        if k < 4:
            for w in W:
                taken(piece(w, tok_of(y, zm, c), x), zr.at[w, zm])
                if k < 3: z_send(w, zm, 1)
        for w in W:
            x_send(w, zp)
            if k < 4: x_send(w, zm)
    def joins(k):
        for w in W: join(w, ring(z, -k, NZ))
        if 0 < k < 4:
            for w in W: join(w, lax.rem(z + k, NZ))

    sgn = 1 - 2 * c
    u = jnp.where(c == 0, x, 3 - x)
    at_u = lambda v: jnp.where(c == 0, v, 3 - v)
    far = a - sgn
    linked = (far >= 0) & (far < n_tok)
    fidx = lambda uu, at: (at_u(uu) - at_u(at)) - 1 + 8 * c
    hb = BLK // 2
    top, bot = pl.ds(0, hb), pl.ds(hb, hb)
    def cross(xx, k):
        @pl.when((xx - x) * sgn > 0)
        def _():
            remote(window_ref.at[widx(xx, x)], window_ref.at[xx - x - 1 + 8 * c], ns.at[k], nr.at[k], sib, x).start()
    def outer_on():
        @pl.when(linked & (u >= 1))
        def _():
            taken(outer_ref, os.at[1])
            remote(outer_ref, window_ref.at[fidx(u, u - 1)], fs.at[0], fr.at[0], a, at_u(u - 1)).start()
        @pl.when(linked & (u == 3))
        def _():
            remote(outer_ref, window_ref.at[fidx(3, 0)], fs.at[1], fr.at[1], a, at_u(0)).start()
    def outer_relay():
        @pl.when(linked & (u <= 2))
        def _():
            taken(window_ref.at[fidx(u + 1, u)], fr.at[0])
        @pl.when(linked & (u >= 1) & (u <= 2))
        def _():
            remote(window_ref.at[fidx(u + 1, u)], window_ref.at[fidx(u + 1, u - 1)], fs.at[2], fr.at[2], a, at_u(u - 1)).start()
    def ring_relay():
        taken(window_ref.at[widx(xm, x)], tr.at[0])
        remote(window_ref.at[widx(xm, x), top], window_ref.at[widx(xm, xp), top], us.at[0], ur.at[0], a, xp).start()
        taken(window_ref.at[widx(xp, x)], tr.at[1])
        remote(window_ref.at[widx(xp, x), bot], window_ref.at[widx(xp, xm), bot], us.at[1], ur.at[1], a, xm).start()
        cross(xm, 0); cross(xp, 1)

    mine = pl.ds(a * 3, 3)
    def send_pages(lo, hi):
        if not do["pages"]: return
        def one(j, _):
            peer = lax.rem(a + lax.rem(j * 27, n_tok), n_tok)
            remote(slots_ref.at[pl.ds(peer * 3, 3)], slots_out.at[mine], ps.at[0], pr.at[0], peer, x).start()
            remote(place_ref.at[peer], place_out.at[a], ps.at[1], pr.at[1], peer, x).start()
            return 0
        lax.fori_loop(lo, hi, one, 0)

    if do["weights"]:
        for w in W:
            pltpu.make_async_copy(shard[w], piece(w, a, x), loc.at[w]).start()
            z_send(w, z, 0, shard[w]); z_send(w, z, 1, shard[w])
            x_send(w, z, shard[w])
    if do["tokens"]:
        pltpu.make_async_copy(tok_ref, window_ref.at[3], loc.at[2]).start()
        @pl.when(linked & (u <= 2))
        def _(): remote(tok_ref, outer_ref, os.at[0], os.at[1], far, x).start()
        remote(tok_ref, window_ref.at[widx(x, xp)], ts.at[0], tr.at[0], a, xp).start()
        remote(tok_ref, window_ref.at[widx(x, xm)], ts.at[1], tr.at[1], a, xm).start()
    if do["pages"]:
        pltpu.make_async_copy(slots_ref.at[mine], slots_out.at[mine], loc.at[3]).start()
        pltpu.make_async_copy(place_ref.at[a], place_out.at[a], loc.at[4]).start()
    send_pages(CUT[0], CUT[1])
    if do["weights"]:
        for w in W: pltpu.make_async_copy(shard[w], piece(w, a, x), loc.at[w]).wait()
        z_step(1); joins(0)
    send_pages(CUT[1], CUT[2])
    if do["weights"]:
        z_step(2); joins(1)
    send_pages(CUT[2], CUT[3])
    if do["weights"]: z_step(3)
    if do["tokens"]: outer_on()
    send_pages(CUT[3], CUT[4])
    if do["weights"]:
        joins(2); z_step(4)
    send_pages(CUT[4], CUT[5])
    if do["tokens"]: ring_relay()
    if do["weights"]:
        joins(3)
    order = lambda i: lax.rem(z + jnp.where(lax.rem(i, 2) == 1, NZ - (i + 1) // 2, i // 2), NZ)
    def relays(lo, hi):
        def relay(i, _):
            for w in W: y_relay(w, order(i))
            return 0
        lax.fori_loop(lo, hi, relay, 0)
    if do["weights"]:
        relays(0, 2)
        joins(4)
    if do["tokens"]: outer_relay()
    if do["weights"]: relays(2, 5)
    if do["tokens"]:
        taken(window_ref.at[widx(xo, x), top], ur.at[0])
        taken(window_ref.at[widx(xo, x), bot], ur.at[1])
        cross(xo, 2)
    if do["weights"]:
        relays(5, NZ)
        def last(i, _):
            for w in W: y_last(w, order(i))
            return 0
        lax.fori_loop(0, NZ, last, 0)
        def sibs(i, _):
            yy, zz = i // NZ, lax.rem(i, NZ)
            for w in W:
                taken(block(w, tok_of(yy, zz, 1 - c)), br.at[w, yy, zz])
                left(block(w, tok_of(yy, zz, c)), bs.at[w, yy, zz])
            return 0
        lax.fori_loop(0, NY * NZ, sibs, 0)
        def drain(zz, _):
            for w in W:
                for d in range(2):
                    left(block(w, a), ys.at[w, d, zz])
                    left(half(w, a, 0), hs.at[w, d, zz])
                for d in range(3):
                    left(piece(w, a, x), xs.at[w, d, zz])
            return 0
        lax.fori_loop(0, NZ, drain, 0)
        for k in range(4):
            for w in W:
                left(piece(w, a, x), zs.at[w, 0, ring(z, -k, NZ)])
                if k < 3: left(piece(w, a, x), zs.at[w, 1, lax.rem(z + k, NZ)])
    if do["tokens"]:
        blk = window_ref.at[3]
        hv = window_ref.at[3, top]
        for d in range(2):
            left(blk, ts.at[d]); left(hv, us.at[d])
        pltpu.make_async_copy(tok_ref, window_ref.at[3], loc.at[2]).wait()
        for k, xx in enumerate((xm, xp, xo)):
            @pl.when((xx - x) * sgn > 0)
            def _(): left(blk, ns.at[k])
            @pl.when((xx - x) * sgn < 0)
            def _(): taken(window_ref.at[xx - x + 7 - 8 * c], nr.at[k])
        @pl.when(linked & (u <= 2))
        def _(): left(blk, os.at[0])
        @pl.when(linked & (u >= 1))
        def _(): left(blk, fs.at[0])
        @pl.when(linked & (u == 3))
        def _(): left(blk, fs.at[1])
        @pl.when(linked & (u >= 1) & (u <= 2))
        def _(): left(blk, fs.at[2])
        @pl.when(linked & (u == 0))
        def _(): taken(window_ref.at[fidx(3, 0)], fr.at[1])
        @pl.when(linked & (u <= 1))
        def _(): taken(window_ref.at[fidx(u + 2, u)], fr.at[2])
    if do["pages"]:
        pltpu.make_async_copy(slots_ref.at[mine], slots_out.at[mine], loc.at[3]).wait()
        pltpu.make_async_copy(place_ref.at[a], place_out.at[a], loc.at[4]).wait()
        rest = pl.ds(0, (n_tok - 1) * 3)
        prest = pl.ds(0, n_tok - 1)
        remote(slots_ref.at[rest], slots_out.at[rest], ps.at[0], pr.at[0], a, xp).wait()
        remote(place_ref.at[prest], place_out.at[prest], ps.at[1], pr.at[1], a, xp).wait()

def comm(tokens, w_in, w_out, slots, place):
    D_ = pltpu.SemaphoreType.DMA
    return pl.pallas_call(
        comm_kernel,
        out_shape=(jax.ShapeDtypeStruct((1024, 3072), BF), jax.ShapeDtypeStruct((1024, 1024), BF),
                   jax.ShapeDtypeStruct((7, tokens.shape[0], 1024), BF),
                   jax.ShapeDtypeStruct(slots.shape, BF), jax.ShapeDtypeStruct(place.shape, place.dtype),
                   jax.ShapeDtypeStruct(tokens.shape, BF)),
        in_specs=[ANY] * 5, out_specs=[ANY] * 6,
        scratch_shapes=[D_((2, 3, NZ)), D_((2, 3, NZ)), D_((2, 2, NZ)), D_((2, NZ)), D_((2, 2, NZ)), D_((2, 2, NZ)),
                        D_((2, 2, NZ)), D_((2, 2, NZ)), D_((2, NY, NZ)), D_((2, NY, NZ)), D_((2,)), D_((2,)), D_((2,)), D_((2,)),
                        D_((3,)), D_((3,)), D_((2,)), D_((3,)), D_((3,)), D_((2,)), D_((2,)), D_((5,))],
        compiler_params=pltpu.CompilerParams(collective_id=0, has_side_effects=True),
    )(tokens, w_in, w_out, slots, place)[:5]


def per_device(tokens, norm_gain, input_weight, output_weight, segment_ids, page_owner, tables):
    device = lax.axis_index("tok") * 4 + lax.axis_index("grp")
    first_row = device * BLK
    ahead = SPAN + REACH * BLK
    padded = jnp.concatenate([
        jnp.full((ahead,), -1, jnp.int32), segment_ids, jnp.full((REACH * BLK + EXTRA,), TOP, jnp.int32)])
    ids = lax.dynamic_slice_in_dim(padded, first_row, SPAN + WIN + EXTRA, 0)
    reach = ids[SPAN : SPAN + WIN]
    own = reach[REACH * BLK : (REACH + 1) * BLK].reshape(3, 128)
    begin = jnp.sum((reach[None, :] < own[:, :1]).astype(jnp.int32), axis=1) // 128
    end = (jnp.sum((reach[None, :] <= own[:, 127:]).astype(jnp.int32), axis=1) + 127) // 128
    bounds = jnp.concatenate([begin, end, first_row[None], first_row[None]])
    ids_row = ids[None, :]
    slots, info = build_slots(tokens, page_owner.reshape(1, -1), ids_row)
    wqkv, wo, window, slots, info = comm(tokens, input_weight, output_weight, slots.reshape(N_TOK * CAP, 8, 512), info)
    return main_call(bounds, window.reshape(WIN, D), wqkv, wo, ids_row, norm_gain[None, :], tables,
                     slots.reshape(N_TOK * CAP * 8, 512), info)


def solution(mesh):
    placed = (
        P(("tok", "grp"), None),
        P(),
        P("tok", "grp"),
        P("tok", "grp"),
        P(),
        P(("tok", "grp"), None),
        P(),
    )
    tables = rope_tables()
    step = jax.shard_map(
        per_device,
        mesh=mesh,
        in_specs=placed,
        out_specs=(P(("tok", "grp"), None), P(("tok", "grp"), None)),
        check_vma=False,
    )
    return lambda *args: step(*args, jnp.asarray(tables))
```
